128 devices in a mesh: section: 2 (over core), row: 32 (over z, y, x_hi), col: 2 (over x_lo).
Axes of the slice: x: 4 (x_hi: 2, x_lo: 2; x = x_hi * 2 + x_lo), y: 4, z: 4, core: 2. Of those that a mesh axis runs over, the one named last changes fastest.
Arguments:
- latents: bfloat16 [32, 4, 256, 1152], P('row', None, 'col'), may hold values from -6 to 6
- timesteps: int32 [32], P('row'), may hold values from 0 to 999
- lengths: int32 [32], P('row'), may hold values from 1 to 1024, 24576 in all
- patch_order: int32 [4], replicated, may hold values from 0 to 3, each once
- ada_weight: bfloat16 [2, 1152, 6, 1152], P('section', 'row', None, 'col'), may hold values from -0.1875 to 0.1875
- qkv_weight: bfloat16 [2, 1152, 3, 1152], P('section', 'row', None, 'col'), may hold values from -1 to 1
- out_weight: bfloat16 [2, 1152, 1152], P('section', 'col', 'row'), may hold values from -0.1875 to 0.1875
- up_weight: bfloat16 [2, 1152, 4608], P('section', 'row', 'col'), may hold values from -0.1875 to 0.1875
- down_weight: bfloat16 [2, 4608, 1152], P('section', 'col', 'row'), may hold values from -0.09375 to 0.09375
- stale_keys: bfloat16 [2, 32, 4, 256, 1152], P('section', 'row', None, None, 'col'), may hold values from -9 to 9
- stale_values: bfloat16 [2, 32, 4, 256, 1152], P('section', 'row', None, None, 'col'), may hold values from -6 to 6
Outputs:
- section_out: bfloat16 [2, 32, 4, 256, 1152], P('section', 'row', None, 'col')
The draws below stay inside these ranges and needn't reach their ends.
Inputs may be any that keep to these rules, and one draw needn't show every extreme that they name: `lengths`: tokens that serve as keys in each request; some request has all 1024. `patch_order`: each of the 4 patches once.
All inputs are finite; a program needn't handle non-finite values. No bound on the sum of `lengths` on one device may be relied on, other than what follows from the above.
Results may differ from the reference program's by a relative error of at most 0.0095.
Values may be sent and summed in bfloat16 or wider, within the bound.
A program may use at most 128 MiB of HBM per device.

```python
import math
import jax
import jax.numpy as jnp
import numpy as np
from jax import lax

D = 1152
HEADS = 16
HD = 72
FF = 4608
SEQ = 1024
PATCHES = 4
PTOK = 256
SECTIONS = 2
REQUESTS = 32
TSTEPS = 1000
N_COL = 2


def width_signs(key):
    return jax.random.randint(jax.random.fold_in(key, 11), (D,), 0, 2).astype(jnp.float32) * 2.0 - 1.0


def head_signs(key):
    return jax.random.randint(jax.random.fold_in(key, 12), (SECTIONS, HEADS, HD), 0, 2).astype(jnp.float32) * 2.0 - 1.0


def head_strength(key):
    offsets = jax.random.randint(jax.random.fold_in(key, 13), (SECTIONS, 1), 0, HEADS)
    ranks = (jnp.arange(HEADS, dtype=jnp.int32)[None, :] * 5 + offsets) % HEADS
    share = ranks.astype(jnp.float32) / (max(HEADS - 1, 1) * 1.0)
    return 0.5 * jnp.exp(share * math.log(160.0))


def draw_latents(key, part):
    shape = (REQUESTS, PATCHES, PTOK, D)
    noise = jax.random.truncated_normal(jax.random.fold_in(key, 21), -4.0, 4.0, shape, jnp.float32)
    amount = jax.random.uniform(jax.random.fold_in(key, 22), (REQUESTS, PATCHES, PTOK, 1), jnp.float32, 0.4, 1.6)
    return (noise + amount * width_signs(key)).astype(jnp.bfloat16)


def draw_qkv_weight(key, part):
    shape = (SECTIONS, D, 3, D)
    spread = 1.0 / math.sqrt(D)
    noise = jax.random.truncated_normal(jax.random.fold_in(key, 31), -4.0, 4.0, shape, jnp.float32) * spread
    columns = (head_strength(key)[:, :, None] * head_signs(key)).reshape(SECTIONS, 1, D)
    planted = columns * width_signs(key)[None, :, None] / (D * math.sqrt(HD))
    which = (jnp.arange(3, dtype=jnp.int32) == 0).astype(jnp.float32)
    return (noise + planted[:, :, None, :] * which[None, None, :, None]).astype(jnp.bfloat16)


def draw_stale_keys(key, part):
    shape = (SECTIONS, REQUESTS, PATCHES, PTOK, HEADS, HD)
    noise = jax.random.truncated_normal(jax.random.fold_in(key, 41), -5.0, 5.0, shape, jnp.float32)
    share = jax.random.uniform(jax.random.fold_in(key, 42), (SECTIONS, REQUESTS, PATCHES, PTOK, HEADS, 1), jnp.float32, 0.0, 1.0)
    lift = 4.0
    keys = noise + lift * share * head_signs(key)[:, None, None, None, :, :]
    return keys.reshape(SECTIONS, REQUESTS, PATCHES, PTOK, D).astype(jnp.bfloat16)


def touch_ends(values, key, smallest, top_value):
    shape = values.shape
    index_at = [jax.random.randint(jax.random.fold_in(key, axis), (), 0, shape[axis]) for axis in range(len(shape))]
    values = values.at[tuple(index_at)].set(smallest)
    longest = shape.index(max(shape))
    index_at[longest] = (index_at[longest] + 1) % shape[longest]
    return values.at[tuple(index_at)].set(top_value)


def levels(key, shape, cuts, low, top_value):
    level = 1.0
    for dim, blocks in cuts:
        draws = jax.random.uniform(jax.random.fold_in(jax.random.fold_in(key, 6), dim), (blocks,), jnp.float32, low / len(cuts), top_value / len(cuts))
        level = level * jnp.repeat(jnp.exp(draws), shape[dim] // blocks).reshape((-1,) + (1,) * (len(shape) - 1 - dim))
    return level


def split_up(count, total, most, lean):
    loads = [(1 << 20) // math.isqrt(grade ** lean) + 1 for grade in range(2, count + 1)]
    rest, given = total - most - (count - 1), [1] * (count - 1)
    while rest > 0:
        free = [i for i in range(count - 1) if given[i] < most]
        pool, budget = sum([loads[i] for i in free]), rest
        for i in free:
            extra = min(most - given[i], max(1, budget * loads[i] // pool), rest)
            given[i] = given[i] + extra
            rest = rest - extra
    return np.array([most] + given)


def uneven_parts(rng, count, total, reach, lean):
    if count == 2:
        one = jax.random.randint(rng, (), max(1, total - reach), min(reach, total - 1) + 1)
        return jnp.stack([one, total - one])
    sizes = jnp.asarray(split_up(count, total, reach, lean), jnp.int32)
    couples = (count - 1) // 2
    source_of, taker = sizes[1:1 + 2 * couples:2], sizes[2:2 + 2 * couples:2]
    slack = jnp.minimum(source_of - 1, reach - taker)
    passed = jax.random.randint(jax.random.fold_in(rng, 1), (couples,), 0, 1 << 20) % (slack + 1)
    sizes = sizes.at[1:1 + 2 * couples:2].set(source_of - passed).at[2:2 + 2 * couples:2].set(taker + passed)
    return sizes[jax.random.permutation(jax.random.fold_in(rng, 2), count)]


def normal_values(own_key, dims, scale, bound, shards=(), kind=jnp.bfloat16):
    values = scale * jax.random.normal(own_key, dims, jnp.float32)
    if shards:
        values = values * levels(own_key, dims, shards, -0.22, 0.18)
    return jnp.clip(values, -bound, bound).astype(kind)


def setup_inputs(seed: int = 0) -> dict:
    arg_keys = jax.random.split(jax.random.key(seed), 12)
    return {
        "latents": draw_latents(jax.random.fold_in(arg_keys[11], 71), 0),
        "timesteps": touch_ends(jax.random.randint(arg_keys[1], (REQUESTS,), 0, TSTEPS), jax.random.fold_in(arg_keys[1], 1), 0, TSTEPS - 1).astype(jnp.int32),
        "lengths": uneven_parts(arg_keys[2], REQUESTS, REQUESTS * SEQ * 3 // 4, SEQ, 2).astype(jnp.int32),
        "patch_order": jax.random.permutation(arg_keys[3], PATCHES).astype(jnp.int32),
        "ada_weight": normal_values(arg_keys[4], (SECTIONS, D, 6, D), D ** -0.5, 0.1875, ((0, 2), (1, 32), (3, 2))),
        "qkv_weight": draw_qkv_weight(jax.random.fold_in(arg_keys[11], 71), 0),
        "out_weight": normal_values(arg_keys[6], (SECTIONS, D, D), D ** -0.5, 0.1875, ((0, 2), (1, 2), (2, 32))),
        "up_weight": normal_values(arg_keys[7], (SECTIONS, D, FF), D ** -0.5, 0.1875, ((0, 2), (1, 32), (2, 2))),
        "down_weight": normal_values(arg_keys[8], (SECTIONS, FF, D), FF ** -0.5, 0.09375, ((0, 2), (1, 2), (2, 32))),
        "stale_keys": draw_stale_keys(jax.random.fold_in(arg_keys[11], 71), 0),
        "stale_values": normal_values(arg_keys[10], (SECTIONS, REQUESTS, PATCHES, PTOK, D), 1.0, 6.0, ((0, 2), (1, 32), (4, 2))),
    }


def sinusoid(step_ids):
    half_width = D // 2
    frequency = jnp.exp(-math.log(10000.0) * jnp.arange(half_width, dtype=jnp.float32) / half_width)
    angles = step_ids.astype(jnp.float32)[:, None] * frequency[None, :]
    return jnp.concatenate([jnp.cos(angles), jnp.sin(angles)], axis=1)

def layer_norm(inputs):
    center = lax.optimization_barrier(jnp.mean(inputs, axis=-1, keepdims=True))
    spread = lax.optimization_barrier(jnp.mean(jnp.square(inputs - center), axis=-1, keepdims=True))
    return (inputs - center) * lax.rsqrt(spread + 1e-06)

def attend(queries, keys, values, valid_keys):
    scores = jnp.einsum('bqhd,bkhd->bhqk', queries.astype(jnp.float32), keys.astype(jnp.float32)) / math.sqrt(HD)
    scores = jnp.where(valid_keys[:, None, None, :], scores, -1e+30)
    top_score = lax.optimization_barrier(jnp.max(scores, axis=-1, keepdims=True))
    weights = jnp.exp(scores - top_score)
    totals = lax.optimization_barrier(jnp.sum(weights, axis=-1))
    probs = weights.astype(jnp.bfloat16)
    mixed = jnp.einsum('bhqk,bkhd->bqhd', probs.astype(jnp.float32), values.astype(jnp.float32))
    return (mixed / jnp.transpose(totals, (0, 2, 1))[..., None]).astype(jnp.bfloat16)

def grouped_sum(inputs, weight):
    requests, tokens, inner = inputs.shape
    group_width = inner // N_COL
    parts = jnp.einsum('rtgc,gcd->grtd', inputs.reshape(requests, tokens, N_COL, group_width).astype(jnp.float32), weight.reshape(N_COL, group_width, weight.shape[1]).astype(jnp.float32))
    rounded = lax.optimization_barrier(parts.astype(jnp.bfloat16)).astype(jnp.float32)
    return lax.optimization_barrier(jnp.sum(rounded, axis=0))

def run_section(section_in, cond, ada, qkv_w, out_w, up_w, down_w, key_cache, value_cache, valid_keys, patch_order):
    modulation = jnp.einsum('rd,dkc->rkc', cond.astype(jnp.float32), ada.astype(jnp.float32))
    shift_attn = modulation[:, 0][:, None, :]
    scale_attn = modulation[:, 1][:, None, :]
    gate_attn = modulation[:, 2][:, None, :]
    shift_mlp = modulation[:, 3][:, None, :]
    scale_mlp = modulation[:, 4][:, None, :]
    gate_mlp = modulation[:, 5][:, None, :]
    requests = section_in.shape[0]
    results = section_in
    for position in range(PATCHES):
        patch_id = patch_order[position]
        tokens_in = lax.dynamic_index_in_dim(section_in, patch_id, 1, keepdims=False).astype(jnp.float32)
        normed = (layer_norm(tokens_in) * (1.0 + scale_attn) + shift_attn).astype(jnp.bfloat16)
        projected = jnp.einsum('rtd,dkc->rtkc', normed.astype(jnp.float32), qkv_w.astype(jnp.float32)).astype(jnp.bfloat16)
        key_cache = lax.dynamic_update_index_in_dim(key_cache, projected[:, :, 1], patch_id, 1)
        value_cache = lax.dynamic_update_index_in_dim(value_cache, projected[:, :, 2], patch_id, 1)
        attended = attend(projected[:, :, 0].reshape(requests, PTOK, HEADS, HD), key_cache.reshape(requests, SEQ, HEADS, HD), value_cache.reshape(requests, SEQ, HEADS, HD), valid_keys).reshape(requests, PTOK, D)
        after_attn = tokens_in + gate_attn * grouped_sum(attended, out_w)
        normed_mlp = (layer_norm(after_attn) * (1.0 + scale_mlp) + shift_mlp).astype(jnp.bfloat16)
        hidden = jax.nn.gelu(jnp.einsum('rtd,df->rtf', normed_mlp.astype(jnp.float32), up_w.astype(jnp.float32)), approximate=True).astype(jnp.bfloat16)
        result = (after_attn + gate_mlp * grouped_sum(hidden, down_w)).astype(jnp.bfloat16)
        results = lax.dynamic_update_index_in_dim(results, result, patch_id, 1)
    return results

def reference(latents, timesteps, lengths, patch_order, ada_weight, qkv_weight, out_weight, up_weight, down_weight, stale_keys, stale_values):
    cond = jax.nn.silu(sinusoid(timesteps)).astype(jnp.bfloat16)
    valid_keys = jnp.arange(SEQ, dtype=jnp.int32)[None, :] < lengths[:, None]
    first = run_section(latents, cond, ada_weight[0], qkv_weight[0], out_weight[0], up_weight[0], down_weight[0], stale_keys[0], stale_values[0], valid_keys, patch_order)
    second = run_section(first, cond, ada_weight[1], qkv_weight[1], out_weight[1], up_weight[1], down_weight[1], stale_keys[1], stale_values[1], valid_keys, patch_order)
    return jnp.stack([first, second])
```

```python
import math

import jax
import jax.numpy as jnp
from jax import lax
from jax.experimental import pallas as pl
from jax.experimental.pallas import tpu as pltpu
from jax.sharding import PartitionSpec as P

D = 1152
HD = 72
F32 = jnp.float32
BF16 = jnp.bfloat16

HEADW = 640
COL_OUT = 3 * HEADW
COL_UP = 4 * HEADW
COL_DOWN = COL_UP + 2304
COLS = COL_DOWN + 2304
QUARTER = COLS // 4
CHUNKS = ((0, COL_UP), (COL_UP, COL_DOWN), (COL_DOWN, COLS))
MAIN = 1024
MESH = pl.DeviceIdType.MESH
NT = (((1,), (1,)), ((), ()))


def sinusoid(step_ids):
    half_width = D // 2
    frequency = jnp.exp(-math.log(10000.0) * jnp.arange(half_width, dtype=F32) / half_width)
    angles = step_ids.astype(F32)[:, None] * frequency[None, :]
    return jnp.concatenate([jnp.cos(angles), jnp.sin(angles)], axis=1)


def halves(chunk):
    start, stop = CHUNKS[chunk]
    middle = start + (stop - start) // 2
    return ((start, middle - start), (middle, stop - middle))


def relay(
    valid_ref, mod_ref, lat_ref, stale_k, stale_v, main_ref, rem_ref, out_ref,
    wall, stag, wrem, x, x1, qs, kbuf, vbuf, att, hid, h, pa_own, pa_got, pm_own, pm_got, y,
    local_sem, xh_send, xh_recv, send_sem, recv_sem, col_send, col_recv, pass_send, pass_recv,
):
    sec = lax.axis_index("section")
    row = lax.axis_index("row")
    col = lax.axis_index("col")
    z, yy, xh = row // 8, lax.rem(row // 2, 4), lax.rem(row, 2)

    def at(section=None, zz=None, y_=None, x_=None, c=None):
        s_ = sec if section is None else section
        r_ = ((z if zz is None else zz) * 4 + (yy if y_ is None else y_)) * 2 + (xh if x_ is None else x_)
        return (s_, r_, col if c is None else c)

    y_peer = [lax.rem(yy + d, 4) for d in range(4)]
    z_peer = [lax.rem(z + d, 4) for d in range(4)]
    xh_dev = at(x_=1 - xh)
    col_dev = at(c=1 - col)
    sec_dev = at(section=1 - sec)

    barrier = pltpu.get_barrier_semaphore()
    for dev in (
        [xh_dev, col_dev, sec_dev]
        + [at(y_=y_peer[d]) for d in (1, 2, 3)]
        + [at(zz=z_peer[d]) for d in (1, 2, 3)]
    ):
        pl.semaphore_signal(barrier, inc=1, device_id=dev, device_id_type=MESH)
    pl.semaphore_wait(barrier, 9)

    def rdma(src, dst, s_sem, r_sem, dev):
        return pltpu.make_async_remote_copy(
            src_ref=src, dst_ref=dst, send_sem=s_sem, recv_sem=r_sem, device_id=dev, device_id_type=MESH
        )

    def buf(k):
        return (stag, 16, rem_ref) if k == 0 else (wall, 32, main_ref)

    def span(k, half):
        if k == 0:
            return ((0, QUARTER // 2), (QUARTER // 2, QUARTER // 2))[half]
        return halves(k - 1)[half]

    pieces = range(1 + len(CHUNKS))

    def xh_copy(k):
        ref, rows, src = buf(k)
        c0 = span(k, 0)[0]
        width = span(k, 0)[1] + span(k, 1)[1]
        return rdma(
            src.at[:, pl.ds(c0, width)],
            ref.at[z, yy, pl.ds(xh * rows, rows), pl.ds(c0, width)],
            xh_send.at[k], xh_recv.at[k], xh_dev,
        )

    def xh_arrival(k):
        ref, rows, src = buf(k)
        c0 = span(k, 0)[0]
        width = span(k, 0)[1] + span(k, 1)[1]
        return rdma(
            src.at[:, pl.ds(c0, width)],
            ref.at[z, yy, pl.ds((1 - xh) * rows, rows), pl.ds(c0, width)],
            xh_send.at[k], xh_recv.at[k], xh_dev,
        )

    def block(k, half, phase, zz, y_):
        ref = buf(k)[0]
        c0, width = span(k, half)
        if phase == 0:
            return ref.at[zz, y_, :, pl.ds(c0, width)]
        if half == 0:
            return ref.at[zz, :, :, pl.ds(c0, width)]
        return ref.at[:, y_, :, pl.ds(c0, width)]

    def ring_copy(k, half, phase, d, arrival):
        i = ((phase * 2 + half) * 4 + k) * 3 + d - 1
        along_y = (half == 0) == (phase == 0)
        if along_y:
            dev = at(y_=y_peer[d])
        else:
            dev = at(zz=z_peer[d])
        zz, y_ = z, yy
        if arrival:
            if along_y:
                y_ = y_peer[4 - d]
            else:
                zz = z_peer[4 - d]
        ref = block(k, half, phase, zz, y_)
        return rdma(ref, ref, send_sem.at[i], recv_sem.at[i], dev)

    own_main = pltpu.make_async_copy(main_ref, wall.at[z, yy, pl.ds(xh * 32, 32)], local_sem.at[0])
    own_rem = pltpu.make_async_copy(rem_ref, stag.at[z, yy, pl.ds(xh * 16, 16)], local_sem.at[1])
    own_main.start()
    own_rem.start()
    for k in pieces:
        xh_copy(k).start()

    x_mine = x.at[:, pl.ds(col * 128, 128)]

    @pl.when(sec == 0)
    def _():
        rdma(lat_ref, x_mine, pass_send.at[4], pass_recv.at[4], col_dev).start()
        x[:, pl.ds(col * 128, 128), :] = lat_ref[...]

    kbuf[...] = stale_k[...]
    vbuf[...] = stale_v[...]
    att[...] = jnp.zeros_like(att)

    own_main.wait()
    own_rem.wait()
    for k in pieces:
        xh_arrival(k).wait_recv()
        for half in (0, 1):
            for d in (1, 3, 2):
                ring_copy(k, half, 0, d, False).start()
    for k in pieces:
        for half in (0, 1):
            for d in (1, 2, 3):
                ring_copy(k, half, 0, d, True).wait_recv()
            for d in (1, 3, 2):
                ring_copy(k, half, 1, d, False).start()

    def arrived(k):
        for half in (0, 1):
            for d in (1, 2, 3):
                ring_copy(k, half, 1, d, True).wait_recv()

    arrived(0)
    rows_i = lax.broadcasted_iota(jnp.int32, (128, 512), 0)
    cols_i = lax.broadcasted_iota(jnp.int32, (128, 512), 1)
    for q in range(4):
        pick = jnp.where(
            ((cols_i >> 4) == (rows_i >> 2)) & ((cols_i & 15) == 4 * q + (rows_i & 3)), 1.0, 0.0
        ).astype(BF16)
        for n in range(QUARTER // 256):
            part = stag[:, :, :, n * 256:(n + 1) * 256].reshape(512, 256)
            wrem[:, q * QUARTER + n * 256:q * QUARTER + (n + 1) * 256] = jnp.dot(
                pick, part, preferred_element_type=F32
            ).astype(BF16)

    def norm_rows(load, shift, scale):
        def body(i, carry):
            rows = pl.ds(pl.multiple_of(i * 32, 32), 32)
            v = load(rows)
            mean = jnp.sum(v, axis=-1, keepdims=True) * (1.0 / D)
            v = v - mean
            var = jnp.sum(v * v, axis=-1, keepdims=True) * (1.0 / D)
            normed = v * lax.rsqrt(var + 1e-6)
            h[rows, :] = (normed * (1.0 + scale[...]) + shift[...]).astype(BF16)
            return carry
        lax.fori_loop(0, 8, body, 0)

    def times(lhs_ref, c0, width):
        return jnp.dot(
            lhs_ref[:, :MAIN], wall[:, :, :, pl.ds(c0, width)].reshape(MAIN, width), preferred_element_type=F32
        ) + jnp.dot(lhs_ref[:, MAIN:], wrem[:, pl.ds(c0, width)], preferred_element_type=F32)

    def times_t(load, dst, j, c0, width):
        def body(zz, carry):
            w = wall[zz, :, :, pl.ds(c0, width)].reshape(256, width)
            dst[j, :, pl.ds(pl.multiple_of(zz * 256, 256), 256)] = lax.dot_general(
                load(), w, NT, preferred_element_type=F32
            ).astype(BF16)
            return carry
        lax.fori_loop(0, 4, body, 0)
        dst[j, :, MAIN:] = lax.dot_general(
            load(), wrem[:, pl.ds(c0, width)], NT, preferred_element_type=F32
        ).astype(BF16)

    def col_copy(own, got, j, base):
        return rdma(own.at[j], got.at[j], col_send.at[base + j], col_recv.at[base + j], col_dev)

    def pass_copy(j):
        return rdma(y.at[j], x.at[j], pass_send.at[j], pass_recv.at[j], sec_dev)

    arrived(1)

    @pl.when(sec == 0)
    def _():
        x_theirs = x.at[:, pl.ds((1 - col) * 128, 128)]
        rdma(lat_ref, x_theirs, pass_send.at[4], pass_recv.at[4], col_dev).wait_recv()

    def attend_step(j, carry):
        @pl.when(sec == 1)
        def _():
            pass_copy(j).wait_recv()

        norm_rows(lambda rows: x[j, rows, :].astype(F32), mod_ref.at[0:1], mod_ref.at[1:2])
        qs[...] = times(h, 0, HEADW).astype(BF16)
        kbuf[j] = times(h, HEADW, HEADW).astype(BF16)
        vbuf[j] = times(h, 2 * HEADW, HEADW).astype(BF16)

        def heads(p, c):
            window = pl.ds(pl.multiple_of(p * 128, 128), 256)
            q_win = qs[:, window]
            k_win = kbuf[:, :, window].reshape(1024, 256)
            v_win = vbuf[:, :, window].reshape(1024, 256)
            lane = lax.broadcasted_iota(jnp.int32, (256, 256), 1) - p * 16
            mixed = att[:, window].astype(F32)
            for e in (0, 1):
                mine = (lane >= e * HD) & (lane < (e + 1) * HD)
                scores = lax.dot_general(
                    jnp.where(mine, q_win.astype(F32), 0.0).astype(BF16), k_win, NT, preferred_element_type=F32
                ) * (1.0 / math.sqrt(HD))
                scores = jnp.where(valid_ref[...] > 0, scores, -1e30)
                weights = jnp.exp(scores - jnp.max(scores, axis=-1, keepdims=True))
                totals = jnp.sum(weights, axis=-1, keepdims=True)
                got = jnp.dot(weights.astype(BF16), v_win, preferred_element_type=F32)
                mixed = jnp.where(mine, got / totals, mixed)
            att[:, window] = mixed.astype(BF16)
            return c
        lax.fori_loop(0, 4, heads, 0)
        times_t(lambda: att[...], pa_own, j, COL_OUT, HEADW)
        col_copy(pa_own, pa_got, j, 0).start()
        return carry
    lax.fori_loop(0, 4, attend_step, 0)

    arrived(2)

    def up_step(j, carry):
        col_copy(pa_own, pa_got, j, 0).wait_recv()

        def load(rows):
            v = x[j, rows, :].astype(F32) + mod_ref[2:3] * (
                pa_own[j, rows, :].astype(F32) + pa_got[j, rows, :].astype(F32)
            )
            x1[j, rows, :] = v
            return v
        norm_rows(load, mod_ref.at[3:4], mod_ref.at[4:5])

        def body(n, c):
            u = times(h, pl.multiple_of(COL_UP + n * 256, 256), 256)
            g = 0.5 * u * (1.0 + jnp.tanh(math.sqrt(2.0 / math.pi) * (u + 0.044715 * (u * u * u))))
            hid[j, :, pl.ds(pl.multiple_of(n * 256, 256), 256)] = g.astype(BF16)
            return c
        lax.fori_loop(0, 9, body, 0)
        return carry
    lax.fori_loop(0, 4, up_step, 0)

    arrived(3)

    def finish(j):
        col_copy(pm_own, pm_got, j, 4).wait_recv()

        def body(i, c):
            rows = pl.ds(pl.multiple_of(i * 32, 32), 32)
            y[j, rows, :] = (
                x1[j, rows, :]
                + mod_ref[5:6] * (pm_own[j, rows, :].astype(F32) + pm_got[j, rows, :].astype(F32))
            ).astype(BF16)
            return c
        lax.fori_loop(0, 8, body, 0)

        @pl.when(sec == 0)
        def _():
            pass_copy(j).start()
        out_ref[j] = y[j, pl.ds(col * 128, 128), :]

    def down_step(j, carry):
        times_t(lambda: hid[j], pm_own, j, COL_DOWN, 2304)
        col_copy(pm_own, pm_got, j, 4).start()

        @pl.when(j > 0)
        def _():
            finish(j - 1)
        return carry
    lax.fori_loop(0, 4, down_step, 0)
    finish(3)

    for k in pieces:
        xh_copy(k).wait_send()
        for phase in (0, 1):
            for half in (0, 1):
                for d in (1, 2, 3):
                    ring_copy(k, half, phase, d, False).wait_send()

    def drain(j, c):
        col_copy(pa_own, pa_got, j, 0).wait_send()
        col_copy(pm_own, pm_got, j, 4).wait_send()

        @pl.when(sec == 0)
        def _():
            pass_copy(j).wait_send()
        return c
    lax.fori_loop(0, 4, drain, 0)

    @pl.when(sec == 0)
    def _():
        rdma(lat_ref, x_mine, pass_send.at[4], pass_recv.at[4], col_dev).wait_send()


def run_relay(valid, mod, lat, stale_k, stale_v, main, rem):
    vmem = pl.BlockSpec(memory_space=pltpu.VMEM)
    tokens = (4, 256, D)
    return pl.pallas_call(
        relay,
        out_shape=jax.ShapeDtypeStruct((4, 128, D), BF16),
        in_specs=[vmem] * 7,
        out_specs=vmem,
        scratch_shapes=[
            pltpu.VMEM((4, 4, 64, COLS), BF16),
            pltpu.VMEM((4, 4, 32, QUARTER), BF16),
            pltpu.VMEM((128, COLS), BF16),
            pltpu.VMEM(tokens, BF16),
            pltpu.VMEM(tokens, F32),
            pltpu.VMEM((256, HEADW), BF16),
            pltpu.VMEM((4, 256, HEADW), BF16),
            pltpu.VMEM((4, 256, HEADW), BF16),
            pltpu.VMEM((256, HEADW), BF16),
            pltpu.VMEM((4, 256, 2304), BF16),
            pltpu.VMEM((256, D), BF16),
            pltpu.VMEM(tokens, BF16),
            pltpu.VMEM(tokens, BF16),
            pltpu.VMEM(tokens, BF16),
            pltpu.VMEM(tokens, BF16),
            pltpu.VMEM(tokens, BF16),
            pltpu.SemaphoreType.DMA((2,)),
            pltpu.SemaphoreType.DMA((4,)),
            pltpu.SemaphoreType.DMA((4,)),
            pltpu.SemaphoreType.DMA((48,)),
            pltpu.SemaphoreType.DMA((48,)),
            pltpu.SemaphoreType.DMA((8,)),
            pltpu.SemaphoreType.DMA((8,)),
            pltpu.SemaphoreType.DMA((5,)),
            pltpu.SemaphoreType.DMA((5,)),
        ],
        compiler_params=pltpu.CompilerParams(
            collective_id=0, has_side_effects=True, vmem_limit_bytes=67043328
        ),
    )(valid, mod, lat, stale_k, stale_v, main, rem)


def local(
    latents,
    timesteps,
    lengths,
    patch_order,
    ada_weight,
    qkv_weight,
    out_weight,
    up_weight,
    down_weight,
    stale_keys,
    stale_values,
):
    row = lax.axis_index("row")
    rows = D // 32

    steps = lax.all_gather(timesteps, "row", axis=0, tiled=True)
    cond = jax.nn.silu(sinusoid(steps)).astype(BF16)
    cond = lax.dynamic_slice_in_dim(cond, row * rows, rows, axis=1)
    partial = jnp.einsum("rd,dkc->rkc", cond, ada_weight[0], preferred_element_type=F32)
    mod = lax.psum_scatter(partial, "row", scatter_dimension=0, tiled=True)
    mod = lax.all_gather(mod, "col", axis=2, tiled=True)
    mod = mod.reshape(6, 32, 36)
    mod = jnp.concatenate([mod[:, :, :32].reshape(6, MAIN), mod[:, :, 32:].reshape(6, 128)], axis=1)

    place = jnp.arange(D, dtype=jnp.int32)
    rest = place - MAIN
    source = jnp.where(place < MAIN, (place // 32) * 36 + place % 32, (rest // 4) * 36 + 32 + rest % 4)
    order = (place[:, None] == source[None, :]).astype(BF16)
    lat = jnp.take(latents[0], patch_order, axis=0)
    lat = jnp.einsum("ptd,de->pte", lat, order, preferred_element_type=F32).astype(BF16)

    pad = lambda a, n: jnp.pad(a, ((0, 0), (0, n - a.shape[1])))
    shard = jnp.concatenate(
        [pad(qkv_weight[0, :, i], HEADW) for i in range(3)]
        + [pad(out_weight[0].T, HEADW), up_weight[0], down_weight[0].T],
        axis=1,
    )
    main = shard[:32]
    rem = shard[32:].reshape(4, 4, QUARTER).transpose(1, 0, 2).reshape(16, QUARTER)

    wide = lambda a: jnp.pad(jnp.take(a, patch_order, axis=0), ((0, 0), (0, 0), (0, HEADW - a.shape[2])))
    position = patch_order[:, None] * 256 + jnp.arange(256, dtype=jnp.int32)[None, :]
    valid = (position < lengths[0]).astype(jnp.int32).reshape(1, 1024)

    out = run_relay(valid, mod, lat, wide(stale_keys[0, 0]), wide(stale_values[0, 0]), main, rem)
    out = jnp.einsum("pte,de->ptd", out, order, preferred_element_type=F32).astype(BF16)
    where = jnp.argmax(patch_order[None, :] == jnp.arange(4, dtype=jnp.int32)[:, None], axis=1)
    return jnp.take(out, where, axis=0)[None, None]


def solution(mesh):
    return jax.shard_map(
        local,
        mesh=mesh,
        in_specs=(
            P("row", None, "col", None),
            P("row"),
            P("row"),
            P(),
            P("section", "row", None, "col"),
            P("section", "row", None, "col"),
            P("section", "col", "row"),
            P("section", "row", "col"),
            P("section", "col", "row"),
            P("section", "row", None, None, "col"),
            P("section", "row", None, None, "col"),
        ),
        out_specs=P("section", "row", None, "col", None),
        check_vma=False,
    )
```

```python
import math

import jax
import jax.numpy as jnp
from jax import lax
from jax.experimental import pallas as pl
from jax.experimental.pallas import tpu as pltpu
from jax.sharding import PartitionSpec as P

D = 1152
HD = 72
F32 = jnp.float32
BF16 = jnp.bfloat16

HEADW = 640
COL_OUT = 3 * HEADW
COL_UP = 4 * HEADW
COL_DOWN = COL_UP + 2304
COLS = COL_DOWN + 2304
QUARTER = COLS // 4
MODW = 6 * HEADW
CHUNKS = ((0, COL_UP), (COL_UP, COL_DOWN), (COL_DOWN, COLS))
MAIN = 1024
MESH = pl.DeviceIdType.MESH
NT = (((1,), (1,)), ((), ()))


def sinusoid(step_ids):
    half_width = D // 2
    frequency = jnp.exp(-math.log(10000.0) * jnp.arange(half_width, dtype=F32) / half_width)
    angles = step_ids.astype(F32)[:, None] * frequency[None, :]
    return jnp.concatenate([jnp.cos(angles), jnp.sin(angles)], axis=1)


def halves(chunk):
    start, stop = CHUNKS[chunk]
    middle = start + (stop - start) // 2
    return ((start, middle - start), (middle, stop - middle))


def relay(
    valid_ref, cond_ref, ada_ref, lat_ref, stale_k, stale_v, main_ref, rem_ref, out_ref,
    cbuf, cmat, part, got_z, sum_z, got_y, sum_y, got_x, mod_own, mod_got, mod_ref,
    wall, stag, wrem, x, x1, qs, kbuf, vbuf, att, hid, h, pa_own, pa_got, pm_own, pm_got, y,
    cond_send, cond_recv, sum_send, sum_recv, local_sem, xh_send, xh_recv, send_sem, recv_sem, col_send, col_recv, pass_send, pass_recv,
):
    sec = lax.axis_index("section")
    row = lax.axis_index("row")
    col = lax.axis_index("col")
    z, yy, xh = row // 8, lax.rem(row // 2, 4), lax.rem(row, 2)

    def at(section=None, zz=None, y_=None, x_=None, c=None):
        s_ = sec if section is None else section
        r_ = ((z if zz is None else zz) * 4 + (yy if y_ is None else y_)) * 2 + (xh if x_ is None else x_)
        return (s_, r_, col if c is None else c)

    y_peer = [lax.rem(yy + d, 4) for d in range(4)]
    z_peer = [lax.rem(z + d, 4) for d in range(4)]
    xh_dev = at(x_=1 - xh)
    col_dev = at(c=1 - col)
    sec_dev = at(section=1 - sec)

    barrier = pltpu.get_barrier_semaphore()
    for dev in (
        [xh_dev, col_dev, sec_dev]
        + [at(y_=y_peer[d]) for d in (1, 2, 3)]
        + [at(zz=z_peer[d]) for d in (1, 2, 3)]
    ):
        pl.semaphore_signal(barrier, inc=1, device_id=dev, device_id_type=MESH)
    pl.semaphore_wait(barrier, 9)

    def rdma(src, dst, s_sem, r_sem, dev):
        return pltpu.make_async_remote_copy(
            src_ref=src, dst_ref=dst, send_sem=s_sem, recv_sem=r_sem, device_id=dev, device_id_type=MESH
        )

    def buf(k):
        return (stag, 16, rem_ref) if k == 0 else (wall, 32, main_ref)

    def span(k, half):
        if k == 0:
            return ((0, QUARTER // 2), (QUARTER // 2, QUARTER // 2))[half]
        return halves(k - 1)[half]

    pieces = range(1 + len(CHUNKS))

    def xh_copy(k):
        ref, rows, src = buf(k)
        c0 = span(k, 0)[0]
        width = span(k, 0)[1] + span(k, 1)[1]
        return rdma(
            src.at[:, pl.ds(c0, width)],
            ref.at[z, yy, pl.ds(xh * rows, rows), pl.ds(c0, width)],
            xh_send.at[k], xh_recv.at[k], xh_dev,
        )

    def xh_arrival(k):
        ref, rows, src = buf(k)
        c0 = span(k, 0)[0]
        width = span(k, 0)[1] + span(k, 1)[1]
        return rdma(
            src.at[:, pl.ds(c0, width)],
            ref.at[z, yy, pl.ds((1 - xh) * rows, rows), pl.ds(c0, width)],
            xh_send.at[k], xh_recv.at[k], xh_dev,
        )

    def block(k, half, phase, zz, y_):
        ref = buf(k)[0]
        c0, width = span(k, half)
        if phase == 0:
            return ref.at[zz, y_, :, pl.ds(c0, width)]
        if half == 0:
            return ref.at[zz, :, :, pl.ds(c0, width)]
        return ref.at[:, y_, :, pl.ds(c0, width)]

    def ring_copy(k, half, phase, d, arrival):
        i = ((phase * 2 + half) * 4 + k) * 3 + d - 1
        along_y = (half == 0) == (phase == 0)
        if along_y:
            dev = at(y_=y_peer[d])
        else:
            dev = at(zz=z_peer[d])
        zz, y_ = z, yy
        if arrival:
            if along_y:
                y_ = y_peer[4 - d]
            else:
                zz = z_peer[4 - d]
        ref = block(k, half, phase, zz, y_)
        return rdma(ref, ref, send_sem.at[i], recv_sem.at[i], dev)

    own_main = pltpu.make_async_copy(main_ref, wall.at[z, yy, pl.ds(xh * 32, 32)], local_sem.at[0])
    own_rem = pltpu.make_async_copy(rem_ref, stag.at[z, yy, pl.ds(xh * 16, 16)], local_sem.at[1])
    own_cond = pltpu.make_async_copy(cond_ref, cbuf.at[z, yy, pl.ds(xh * 32, 32)], local_sem.at[2])
    own_cond.start()
    cond_xh = rdma(cond_ref, cbuf.at[z, yy, pl.ds(xh * 32, 32)], cond_send.at[0], cond_recv.at[0], xh_dev)
    cond_xh.start()
    own_main.start()
    own_rem.start()
    for k in pieces:
        xh_copy(k).start()

    x_mine = x.at[:, pl.ds(col * 128, 128)]

    @pl.when(sec == 0)
    def _():
        rdma(lat_ref, x_mine, pass_send.at[4], pass_recv.at[4], col_dev).start()
        x[:, pl.ds(col * 128, 128), :] = lat_ref[...]

    kbuf[...] = stale_k[...]
    vbuf[...] = stale_v[...]
    att[...] = jnp.zeros_like(att)

    own_cond.wait()
    rdma(
        cond_ref, cbuf.at[z, yy, pl.ds((1 - xh) * 32, 32)], cond_send.at[0], cond_recv.at[0], xh_dev
    ).wait_recv()

    def cond_y(d, arrival):
        ref = cbuf.at[z, y_peer[4 - d] if arrival else yy]
        return rdma(ref, ref, cond_send.at[d], cond_recv.at[d], at(y_=y_peer[d]))

    def cond_z(d, arrival):
        ref = cbuf.at[z_peer[4 - d] if arrival else z]
        return rdma(ref, ref, cond_send.at[3 + d], cond_recv.at[3 + d], at(zz=z_peer[d]))

    def part_z(d):
        return rdma(part.at[z_peer[d]], got_z.at[d - 1], sum_send.at[d - 1], sum_recv.at[d - 1], at(zz=z_peer[d]))

    def part_y(d):
        return rdma(sum_z.at[y_peer[d]], got_y.at[d - 1], sum_send.at[d + 2], sum_recv.at[d + 2], at(y_=y_peer[d]))

    for d in (1, 3, 2):
        cond_y(d, False).start()
    for d in (1, 3, 2):
        cond_y(d, True).wait_recv()
    for d in (1, 3, 2):
        cond_z(d, False).start()
    for d in (1, 3, 2):
        cond_z(d, True).wait_recv()
    for i in range(32):
        cmat[i:i + 1, :] = cbuf[i // 8, (i // 2) % 4, pl.ds((i % 2) * 32 + row, 1), :]
    products = jnp.dot(cmat[...].astype(BF16), ada_ref[...], preferred_element_type=F32)
    for i in range(32):
        part[i // 8, (i // 2) % 4, i % 2] = products[i:i + 1, :]
    for d in (1, 3, 2):
        part_z(d).start()
    for d in (1, 3, 2):
        part_z(d).wait_recv()
    sum_z[...] = part[z] + got_z[0] + got_z[1] + got_z[2]
    for d in (1, 3, 2):
        part_y(d).start()
    for d in (1, 3, 2):
        part_y(d).wait_recv()
    sum_y[...] = sum_z[yy] + got_y[0] + got_y[1] + got_y[2]
    part_x = rdma(sum_y.at[1 - xh], got_x, sum_send.at[6], sum_recv.at[6], xh_dev)
    part_x.start()
    part_x.wait_recv()
    mod_own[...] = sum_y[xh] + got_x[...]
    mod_copy = rdma(mod_own, mod_got, sum_send.at[7], sum_recv.at[7], col_dev)
    mod_copy.start()

    own_main.wait()
    own_rem.wait()
    for k in pieces:
        xh_arrival(k).wait_recv()
        for half in (0, 1):
            for d in (1, 3, 2):
                ring_copy(k, half, 0, d, False).start()
    for k in pieces:
        for half in (0, 1):
            for d in (1, 2, 3):
                ring_copy(k, half, 0, d, True).wait_recv()
            for d in (1, 3, 2):
                ring_copy(k, half, 1, d, False).start()

    def arrived(k):
        for half in (0, 1):
            for d in (1, 2, 3):
                ring_copy(k, half, 1, d, True).wait_recv()

    mod_copy.wait_recv()
    for k in range(6):
        base = k * HEADW
        mod_ref[k:k + 1, pl.ds(col * 512, 512)] = mod_own[:, base:base + 512]
        mod_ref[k:k + 1, pl.ds((1 - col) * 512, 512)] = mod_got[:, base:base + 512]
        mod_ref[k:k + 1, MAIN:] = mod_own[:, base + 512:base + HEADW] + mod_got[:, base + 512:base + HEADW]

    arrived(0)
    rows_i = lax.broadcasted_iota(jnp.int32, (128, 512), 0)
    cols_i = lax.broadcasted_iota(jnp.int32, (128, 512), 1)
    for q in range(4):
        pick = jnp.where(
            ((cols_i >> 4) == (rows_i >> 2)) & ((cols_i & 15) == 4 * q + (rows_i & 3)), 1.0, 0.0
        ).astype(BF16)
        for n in range(QUARTER // 256):
            rest = stag[:, :, :, n * 256:(n + 1) * 256].reshape(512, 256)
            wrem[:, q * QUARTER + n * 256:q * QUARTER + (n + 1) * 256] = jnp.dot(
                pick, rest, preferred_element_type=F32
            ).astype(BF16)

    def norm_rows(load, shift, scale):
        def body(i, carry):
            rows = pl.ds(pl.multiple_of(i * 32, 32), 32)
            v = load(rows)
            mean = jnp.sum(v, axis=-1, keepdims=True) * (1.0 / D)
            v = v - mean
            var = jnp.sum(v * v, axis=-1, keepdims=True) * (1.0 / D)
            normed = v * lax.rsqrt(var + 1e-6)
            h[rows, :] = (normed * (1.0 + scale[...]) + shift[...]).astype(BF16)
            return carry
        lax.fori_loop(0, 8, body, 0)

    def times(lhs_ref, c0, width):
        return jnp.dot(
            lhs_ref[:, :MAIN], wall[:, :, :, pl.ds(c0, width)].reshape(MAIN, width), preferred_element_type=F32
        ) + jnp.dot(lhs_ref[:, MAIN:], wrem[:, pl.ds(c0, width)], preferred_element_type=F32)

    def times_t(load, dst, j, c0, width):
        def body(zz, carry):
            w = wall[zz, :, :, pl.ds(c0, width)].reshape(256, width)
            dst[j, :, pl.ds(pl.multiple_of(zz * 256, 256), 256)] = lax.dot_general(
                load(), w, NT, preferred_element_type=F32
            ).astype(BF16)
            return carry
        lax.fori_loop(0, 4, body, 0)
        dst[j, :, MAIN:] = lax.dot_general(
            load(), wrem[:, pl.ds(c0, width)], NT, preferred_element_type=F32
        ).astype(BF16)

    def col_copy(own, got, j, base):
        return rdma(own.at[j], got.at[j], col_send.at[base + j], col_recv.at[base + j], col_dev)

    def pass_copy(j):
        return rdma(y.at[j], x.at[j], pass_send.at[j], pass_recv.at[j], sec_dev)

    arrived(1)

    @pl.when(sec == 0)
    def _():
        x_theirs = x.at[:, pl.ds((1 - col) * 128, 128)]
        rdma(lat_ref, x_theirs, pass_send.at[4], pass_recv.at[4], col_dev).wait_recv()

    def attend_step(j, carry):
        @pl.when(sec == 1)
        def _():
            pass_copy(j).wait_recv()

        norm_rows(lambda rows: x[j, rows, :].astype(F32), mod_ref.at[0:1], mod_ref.at[1:2])
        qs[...] = times(h, 0, HEADW).astype(BF16)
        kbuf[j] = times(h, HEADW, HEADW).astype(BF16)
        vbuf[j] = times(h, 2 * HEADW, HEADW).astype(BF16)

        def heads(p, c):
            window = pl.ds(pl.multiple_of(p * 128, 128), 256)
            q_win = qs[:, window]
            k_win = kbuf[:, :, window].reshape(1024, 256)
            v_win = vbuf[:, :, window].reshape(1024, 256)
            lane = lax.broadcasted_iota(jnp.int32, (256, 256), 1) - p * 16
            mixed = att[:, window].astype(F32)
            for e in (0, 1):
                mine = (lane >= e * HD) & (lane < (e + 1) * HD)
                scores = lax.dot_general(
                    jnp.where(mine, q_win.astype(F32), 0.0).astype(BF16), k_win, NT, preferred_element_type=F32
                ) * (1.0 / math.sqrt(HD))
                scores = jnp.where(valid_ref[...] > 0, scores, -1e30)
                weights = jnp.exp(scores - jnp.max(scores, axis=-1, keepdims=True))
                totals = jnp.sum(weights, axis=-1, keepdims=True)
                got = jnp.dot(weights.astype(BF16), v_win, preferred_element_type=F32)
                mixed = jnp.where(mine, got / totals, mixed)
            att[:, window] = mixed.astype(BF16)
            return c
        lax.fori_loop(0, 4, heads, 0)
        times_t(lambda: att[...], pa_own, j, COL_OUT, HEADW)
        col_copy(pa_own, pa_got, j, 0).start()
        return carry
    lax.fori_loop(0, 4, attend_step, 0)

    arrived(2)

    def up_step(j, carry):
        col_copy(pa_own, pa_got, j, 0).wait_recv()

        def load(rows):
            v = x[j, rows, :].astype(F32) + mod_ref[2:3] * (
                pa_own[j, rows, :].astype(F32) + pa_got[j, rows, :].astype(F32)
            )
            x1[j, rows, :] = v
            return v
        norm_rows(load, mod_ref.at[3:4], mod_ref.at[4:5])

        def body(n, c):
            u = times(h, pl.multiple_of(COL_UP + n * 256, 256), 256)
            g = 0.5 * u * (1.0 + jnp.tanh(math.sqrt(2.0 / math.pi) * (u + 0.044715 * (u * u * u))))
            hid[j, :, pl.ds(pl.multiple_of(n * 256, 256), 256)] = g.astype(BF16)
            return c
        lax.fori_loop(0, 9, body, 0)
        return carry
    lax.fori_loop(0, 4, up_step, 0)

    arrived(3)

    def finish(j):
        col_copy(pm_own, pm_got, j, 4).wait_recv()

        def body(i, c):
            rows = pl.ds(pl.multiple_of(i * 32, 32), 32)
            y[j, rows, :] = (
                x1[j, rows, :]
                + mod_ref[5:6] * (pm_own[j, rows, :].astype(F32) + pm_got[j, rows, :].astype(F32))
            ).astype(BF16)
            return c
        lax.fori_loop(0, 8, body, 0)

        @pl.when(sec == 0)
        def _():
            pass_copy(j).start()
        out_ref[j] = y[j, pl.ds(col * 128, 128), :]

    def down_step(j, carry):
        times_t(lambda: hid[j], pm_own, j, COL_DOWN, 2304)
        col_copy(pm_own, pm_got, j, 4).start()

        @pl.when(j > 0)
        def _():
            finish(j - 1)
        return carry
    lax.fori_loop(0, 4, down_step, 0)
    finish(3)

    cond_xh.wait_send()
    for d in (1, 2, 3):
        cond_y(d, False).wait_send()
        cond_z(d, False).wait_send()
        part_z(d).wait_send()
        part_y(d).wait_send()
    part_x.wait_send()
    mod_copy.wait_send()
    for k in pieces:
        xh_copy(k).wait_send()
        for phase in (0, 1):
            for half in (0, 1):
                for d in (1, 2, 3):
                    ring_copy(k, half, phase, d, False).wait_send()

    def drain(j, c):
        col_copy(pa_own, pa_got, j, 0).wait_send()
        col_copy(pm_own, pm_got, j, 4).wait_send()

        @pl.when(sec == 0)
        def _():
            pass_copy(j).wait_send()
        return c
    lax.fori_loop(0, 4, drain, 0)

    @pl.when(sec == 0)
    def _():
        rdma(lat_ref, x_mine, pass_send.at[4], pass_recv.at[4], col_dev).wait_send()


def run_relay(valid, cond, ada, lat, stale_k, stale_v, main, rem):
    vmem = pl.BlockSpec(memory_space=pltpu.VMEM)
    tokens = (4, 256, D)
    return pl.pallas_call(
        relay,
        out_shape=jax.ShapeDtypeStruct((4, 128, D), BF16),
        in_specs=[vmem] * 8,
        out_specs=vmem,
        scratch_shapes=[
            pltpu.VMEM((4, 4, 64, 128), F32),
            pltpu.VMEM((32, 128), F32),
            pltpu.VMEM((4, 4, 2, 1, MODW), F32),
            pltpu.VMEM((3, 4, 2, 1, MODW), F32),
            pltpu.VMEM((4, 2, 1, MODW), F32),
            pltpu.VMEM((3, 2, 1, MODW), F32),
            pltpu.VMEM((2, 1, MODW), F32),
            pltpu.VMEM((1, MODW), F32),
            pltpu.VMEM((1, MODW), F32),
            pltpu.VMEM((1, MODW), F32),
            pltpu.VMEM((8, D), F32),
            pltpu.VMEM((4, 4, 64, COLS), BF16),
            pltpu.VMEM((4, 4, 32, QUARTER), BF16),
            pltpu.VMEM((128, COLS), BF16),
            pltpu.VMEM(tokens, BF16),
            pltpu.VMEM(tokens, F32),
            pltpu.VMEM((256, HEADW), BF16),
            pltpu.VMEM((4, 256, HEADW), BF16),
            pltpu.VMEM((4, 256, HEADW), BF16),
            pltpu.VMEM((256, HEADW), BF16),
            pltpu.VMEM((4, 256, 2304), BF16),
            pltpu.VMEM((256, D), BF16),
            pltpu.VMEM(tokens, BF16),
            pltpu.VMEM(tokens, BF16),
            pltpu.VMEM(tokens, BF16),
            pltpu.VMEM(tokens, BF16),
            pltpu.VMEM(tokens, BF16),
            pltpu.SemaphoreType.DMA((7,)),
            pltpu.SemaphoreType.DMA((7,)),
            pltpu.SemaphoreType.DMA((8,)),
            pltpu.SemaphoreType.DMA((8,)),
            pltpu.SemaphoreType.DMA((3,)),
            pltpu.SemaphoreType.DMA((4,)),
            pltpu.SemaphoreType.DMA((4,)),
            pltpu.SemaphoreType.DMA((48,)),
            pltpu.SemaphoreType.DMA((48,)),
            pltpu.SemaphoreType.DMA((8,)),
            pltpu.SemaphoreType.DMA((8,)),
            pltpu.SemaphoreType.DMA((5,)),
            pltpu.SemaphoreType.DMA((5,)),
        ],
        compiler_params=pltpu.CompilerParams(
            collective_id=0, has_side_effects=True, vmem_limit_bytes=67043328
        ),
    )(valid, cond, ada, lat, stale_k, stale_v, main, rem)


def local(
    latents,
    timesteps,
    lengths,
    patch_order,
    ada_weight,
    qkv_weight,
    out_weight,
    up_weight,
    down_weight,
    stale_keys,
    stale_values,
):
    cond = jax.nn.silu(sinusoid(timesteps)).astype(BF16).astype(F32)
    cond = jnp.pad(cond.reshape(32, 36), ((0, 0), (0, 92)))
    from_col = jnp.arange(576, dtype=jnp.int32)
    group, inner = from_col // 36, from_col % 36
    to_col = jnp.where(
        inner < 32, group * 32 + inner, 512 + 64 * lax.axis_index("col") + group * 4 + inner - 32
    )
    spread = (to_col[:, None] == jnp.arange(HEADW, dtype=jnp.int32)[None, :]).astype(BF16)
    ada = jnp.einsum("dkc,ce->dke", ada_weight[0], spread, preferred_element_type=F32).astype(BF16)
    ada = jnp.pad(ada.reshape(36, MODW), ((0, 92), (0, 0)))

    place = jnp.arange(D, dtype=jnp.int32)
    rest = place - MAIN
    source = jnp.where(place < MAIN, (place // 32) * 36 + place % 32, (rest // 4) * 36 + 32 + rest % 4)
    order = (place[:, None] == source[None, :]).astype(BF16)
    lat = jnp.take(latents[0], patch_order, axis=0)
    lat = jnp.einsum("ptd,de->pte", lat, order, preferred_element_type=F32).astype(BF16)

    pad = lambda a, n: jnp.pad(a, ((0, 0), (0, n - a.shape[1])))
    shard = jnp.concatenate(
        [pad(qkv_weight[0, :, i], HEADW) for i in range(3)]
        + [pad(out_weight[0].T, HEADW), up_weight[0], down_weight[0].T],
        axis=1,
    )
    main = shard[:32]
    rem = shard[32:].reshape(4, 4, QUARTER).transpose(1, 0, 2).reshape(16, QUARTER)

    wide = lambda a: jnp.pad(jnp.take(a, patch_order, axis=0), ((0, 0), (0, 0), (0, HEADW - a.shape[2])))
    position = patch_order[:, None] * 256 + jnp.arange(256, dtype=jnp.int32)[None, :]
    valid = (position < lengths[0]).astype(jnp.int32).reshape(1, 1024)

    out = run_relay(valid, cond, ada, lat, wide(stale_keys[0, 0]), wide(stale_values[0, 0]), main, rem)
    out = jnp.einsum("pte,de->ptd", out, order, preferred_element_type=F32).astype(BF16)
    where = jnp.argmax(patch_order[None, :] == jnp.arange(4, dtype=jnp.int32)[:, None], axis=1)
    return jnp.take(out, where, axis=0)[None, None]


def solution(mesh):
    return jax.shard_map(
        local,
        mesh=mesh,
        in_specs=(
            P("row", None, "col", None),
            P("row"),
            P("row"),
            P(),
            P("section", "row", None, "col"),
            P("section", "row", None, "col"),
            P("section", "col", "row"),
            P("section", "row", "col"),
            P("section", "col", "row"),
            P("section", "row", None, None, "col"),
            P("section", "row", None, None, "col"),
        ),
        out_specs=P("section", "row", None, "col", None),
        check_vma=False,
    )
```

```python
import math

import jax
import jax.numpy as jnp
from jax import lax
from jax.experimental import pallas as pl
from jax.experimental.pallas import tpu as pltpu
from jax.sharding import PartitionSpec as P

D = 1152
HD = 72
F32 = jnp.float32
BF16 = jnp.bfloat16

HEADW = 640
COL_OUT = 3 * HEADW
COL_UP = 4 * HEADW
COL_DOWN = COL_UP + 2304
COLS = COL_DOWN + 2304
QUARTER = COLS // 4
MODW = 6 * HEADW
CHUNKS = ((0, COL_UP), (COL_UP, COL_DOWN), (COL_DOWN, COLS))
MAIN = 1024
MESH = pl.DeviceIdType.MESH
NT = (((1,), (1,)), ((), ()))


def sinusoid(step_ids):
    half_width = D // 2
    frequency = jnp.exp(-math.log(10000.0) * jnp.arange(half_width, dtype=F32) / half_width)
    angles = step_ids.astype(F32)[:, None] * frequency[None, :]
    return jnp.concatenate([jnp.cos(angles), jnp.sin(angles)], axis=1)


def halves(chunk):
    start, stop = CHUNKS[chunk]
    middle = start + (stop - start) // 2
    return ((start, middle - start), (middle, stop - middle))


def relay(
    place_ref, slot_ref, length_ref, cond_ref, ada_ref, lat_ref, stale_k, stale_v, main_ref, rem_ref, out_ref,
    order, valid_ref, latp, yout,
    cbuf, cmat, part, got_z, sum_z, got_y, sum_y, got_x, mod_own, mod_got, mod_ref,
    wall, stag, wrem, x, x1, qs, kbuf, vbuf, att, hid, h, pa_own, pa_got, pm_own, pm_got, y,
    cond_send, cond_recv, sum_send, sum_recv, go_sem, local_sem, xh_send, xh_recv, send_sem, recv_sem, col_send, col_recv, pass_send, pass_recv,
):
    sec = lax.axis_index("section")
    row = lax.axis_index("row")
    col = lax.axis_index("col")
    z, yy, xh = row // 8, lax.rem(row // 2, 4), lax.rem(row, 2)

    def at(section=None, zz=None, y_=None, x_=None, c=None):
        s_ = sec if section is None else section
        r_ = ((z if zz is None else zz) * 4 + (yy if y_ is None else y_)) * 2 + (xh if x_ is None else x_)
        return (s_, r_, col if c is None else c)

    y_peer = [lax.rem(yy + d, 4) for d in range(4)]
    z_peer = [lax.rem(z + d, 4) for d in range(4)]
    xh_dev = at(x_=1 - xh)
    col_dev = at(c=1 - col)
    sec_dev = at(section=1 - sec)

    barrier = pltpu.get_barrier_semaphore()
    for dev in (
        [xh_dev, col_dev, sec_dev]
        + [at(y_=y_peer[d]) for d in (1, 2, 3)]
        + [at(zz=z_peer[d]) for d in (1, 2, 3)]
    ):
        pl.semaphore_signal(barrier, inc=1, device_id=dev, device_id_type=MESH)
    pl.semaphore_wait(barrier, 9)

    def rdma(src, dst, s_sem, r_sem, dev):
        return pltpu.make_async_remote_copy(
            src_ref=src, dst_ref=dst, send_sem=s_sem, recv_sem=r_sem, device_id=dev, device_id_type=MESH
        )

    def buf(k):
        return (stag, 16, rem_ref) if k == 0 else (wall, 32, main_ref)

    def span(k, half):
        if k == 0:
            return ((0, QUARTER // 2), (QUARTER // 2, QUARTER // 2))[half]
        return halves(k - 1)[half]

    pieces = range(1 + len(CHUNKS))

    def xh_copy(k):
        ref, rows, src = buf(k)
        c0 = span(k, 0)[0]
        width = span(k, 0)[1] + span(k, 1)[1]
        return rdma(
            src.at[:, pl.ds(c0, width)],
            ref.at[z, yy, pl.ds(xh * rows, rows), pl.ds(c0, width)],
            xh_send.at[k], xh_recv.at[k], xh_dev,
        )

    def xh_arrival(k):
        ref, rows, src = buf(k)
        c0 = span(k, 0)[0]
        width = span(k, 0)[1] + span(k, 1)[1]
        return rdma(
            src.at[:, pl.ds(c0, width)],
            ref.at[z, yy, pl.ds((1 - xh) * rows, rows), pl.ds(c0, width)],
            xh_send.at[k], xh_recv.at[k], xh_dev,
        )

    def ring_copy(k, half, phase, link, arrival):
        i = ((phase * 2 + half) * 4 + k) * 4 + link
        along_y = (half == 0) == (phase == 0)
        ahead = link % 2 == 0
        peers = y_peer if along_y else z_peer
        dev = at(y_=peers[1 if ahead else 3]) if along_y else at(zz=peers[1 if ahead else 3])
        if arrival:
            member = peers[(3 if ahead else 1) if link < 2 else 2]
        else:
            member = peers[0 if link < 2 else (3 if ahead else 1)]
        c0, width = span(k, half)
        if link >= 2:
            first = (width // 256) * 128 if (width // 128) % 2 == 0 else (width // 256 + 1) * 128
            c0, width = (c0, first) if ahead else (c0 + first, width - first)
        ref = buf(k)[0]
        zz, y_ = (z, member) if along_y else (member, yy)
        if phase == 0:
            ref = ref.at[zz, y_, :, pl.ds(c0, width)]
        elif along_y:
            ref = ref.at[:, y_, :, pl.ds(c0, width)]
        else:
            ref = ref.at[zz, :, :, pl.ds(c0, width)]
        return rdma(ref, ref, send_sem.at[i], recv_sem.at[i], dev)

    def near(k, phase):
        for half in (0, 1):
            for link in (0, 1):
                ring_copy(k, half, phase, link, False).start()

    def relay_on(k, phase):
        for half in (0, 1):
            for link in (0, 1):
                ring_copy(k, half, phase, link, True).wait_recv()
                ring_copy(k, half, phase, link + 2, False).start()

    def far_arrived(k, phase):
        for half in (0, 1):
            for link in (2, 3):
                ring_copy(k, half, phase, link, True).wait_recv()

    own_main = pltpu.make_async_copy(main_ref, wall.at[z, yy, pl.ds(xh * 32, 32)], local_sem.at[0])
    own_rem = pltpu.make_async_copy(rem_ref, stag.at[z, yy, pl.ds(xh * 16, 16)], local_sem.at[1])
    own_cond = pltpu.make_async_copy(cond_ref, cbuf.at[z, yy, pl.ds(xh * 32, 32)], local_sem.at[2])
    own_cond.start()
    cond_xh = rdma(cond_ref, cbuf.at[z, yy, pl.ds(xh * 32, 32)], cond_send.at[0], cond_recv.at[0], xh_dev)
    cond_xh.start()
    own_main.start()
    own_rem.start()
    for k in pieces:
        xh_copy(k).start()

    lane = lax.broadcasted_iota(jnp.int32, (128, D), 1)
    rest_lane = lane - MAIN
    source = jnp.where(
        lane < MAIN, (lane >> 5) * 36 + (lane & 31), (rest_lane >> 2) * 36 + 32 + (rest_lane & 3)
    )
    for i in range(9):
        natural = lax.broadcasted_iota(jnp.int32, (128, D), 0) + i * 128
        order[i * 128:(i + 1) * 128, :] = jnp.where(natural == source, 1.0, 0.0).astype(BF16)

    x_mine = x.at[:, pl.ds(col * 128, 128)]

    def lat_copy():
        return rdma(latp, x_mine, pass_send.at[4], pass_recv.at[4], col_dev)

    @pl.when(sec == 0)
    def _():
        for j in range(4):
            latp[j] = jnp.dot(lat_ref[place_ref[j]], order[...], preferred_element_type=F32).astype(BF16)
        lat_copy().start()
        x[:, pl.ds(col * 128, 128), :] = latp[...]

    own_cond.wait()
    rdma(
        cond_ref, cbuf.at[z, yy, pl.ds((1 - xh) * 32, 32)], cond_send.at[0], cond_recv.at[0], xh_dev
    ).wait_recv()

    def cond_y(d, arrival):
        ref = cbuf.at[z, y_peer[4 - d] if arrival else yy]
        return rdma(ref, ref, cond_send.at[d], cond_recv.at[d], at(y_=y_peer[d]))

    def cond_z(d, arrival):
        ref = cbuf.at[z_peer[4 - d] if arrival else z]
        return rdma(ref, ref, cond_send.at[3 + d], cond_recv.at[3 + d], at(zz=z_peer[d]))

    def part_z(d):
        return rdma(part.at[z_peer[d]], got_z.at[d - 1], sum_send.at[d - 1], sum_recv.at[d - 1], at(zz=z_peer[d]))

    def part_y(d):
        return rdma(sum_z.at[y_peer[d]], got_y.at[d - 1], sum_send.at[d + 2], sum_recv.at[d + 2], at(y_=y_peer[d]))

    for d in (1, 3, 2):
        cond_y(d, False).start()
    own_main.wait()
    own_rem.wait()

    @pl.when(sec == 1)
    def _():
        pl.semaphore_wait(go_sem, 1)

    xh_arrival(0).wait_recv()
    near(0, 0)
    xh_arrival(1).wait_recv()
    near(1, 0)
    for d in (1, 3, 2):
        cond_y(d, True).wait_recv()
    for d in (1, 3, 2):
        cond_z(d, False).start()
    for d in (1, 3, 2):
        cond_z(d, True).wait_recv()
    for i in range(32):
        cmat[i:i + 1, :] = cbuf[i // 8, (i // 2) % 4, pl.ds((i % 2) * 32 + row, 1), :]
    products = jnp.dot(cmat[...].astype(BF16), ada_ref[...], preferred_element_type=F32)
    for i in range(32):
        part[i // 8, (i // 2) % 4, i % 2] = products[i:i + 1, :]
    for d in (1, 3, 2):
        part_z(d).start()
    xh_arrival(2).wait_recv()
    near(2, 0)
    xh_arrival(3).wait_recv()
    near(3, 0)
    relay_on(0, 0)
    relay_on(1, 0)
    for d in (1, 3, 2):
        part_z(d).wait_recv()
    sum_z[...] = part[z] + got_z[0] + got_z[1] + got_z[2]
    for d in (1, 3, 2):
        part_y(d).start()
    far_arrived(0, 0)
    near(0, 1)
    relay_on(2, 0)
    relay_on(3, 0)
    for d in (1, 3, 2):
        part_y(d).wait_recv()
    sum_y[...] = sum_z[yy] + got_y[0] + got_y[1] + got_y[2]
    part_x = rdma(sum_y.at[1 - xh], got_x, sum_send.at[6], sum_recv.at[6], xh_dev)
    part_x.start()
    far_arrived(1, 0)
    near(1, 1)
    part_x.wait_recv()
    mod_own[...] = sum_y[xh] + got_x[...]
    mod_copy = rdma(mod_own, mod_got, sum_send.at[7], sum_recv.at[7], col_dev)
    mod_copy.start()
    far_arrived(2, 0)
    far_arrived(3, 0)
    relay_on(0, 1)
    near(2, 1)

    for j in range(4):
        kbuf[j, :, :576] = stale_k[place_ref[j]]
        vbuf[j, :, :576] = stale_v[place_ref[j]]
        kbuf[j, :, 576:] = jnp.zeros((256, HEADW - 576), BF16)
        vbuf[j, :, 576:] = jnp.zeros((256, HEADW - 576), BF16)
        token = lax.broadcasted_iota(jnp.int32, (1, 256), 1) + place_ref[j] * 256
        valid_ref[:, j * 256:(j + 1) * 256] = jnp.where(token < length_ref[0], 1, 0)
    att[...] = jnp.zeros_like(att)

    mod_copy.wait_recv()
    for k in range(6):
        base = k * HEADW
        mod_ref[k:k + 1, pl.ds(col * 512, 512)] = mod_own[:, base:base + 512]
        mod_ref[k:k + 1, pl.ds((1 - col) * 512, 512)] = mod_got[:, base:base + 512]
        mod_ref[k:k + 1, MAIN:] = mod_own[:, base + 512:base + HEADW] + mod_got[:, base + 512:base + HEADW]

    relay_on(1, 1)
    near(3, 1)
    far_arrived(0, 1)
    rows_i = lax.broadcasted_iota(jnp.int32, (128, 512), 0)
    cols_i = lax.broadcasted_iota(jnp.int32, (128, 512), 1)
    for q in range(4):
        pick = jnp.where(
            ((cols_i >> 4) == (rows_i >> 2)) & ((cols_i & 15) == 4 * q + (rows_i & 3)), 1.0, 0.0
        ).astype(BF16)
        wrem[:, q * QUARTER:(q + 1) * QUARTER] = jnp.dot(
            pick, stag[...].reshape(512, QUARTER), preferred_element_type=F32
        ).astype(BF16)

    def norm_rows(load, shift, scale):
        def body(i, carry):
            rows = pl.ds(pl.multiple_of(i * 64, 64), 64)
            v = load(rows)
            mean = jnp.sum(v, axis=-1, keepdims=True) * (1.0 / D)
            v = v - mean
            var = jnp.sum(v * v, axis=-1, keepdims=True) * (1.0 / D)
            normed = v * lax.rsqrt(var + 1e-6)
            h[rows, :] = (normed * (1.0 + scale[...]) + shift[...]).astype(BF16)
            return carry
        lax.fori_loop(0, 4, body, 0, unroll=4)

    def times(lhs_ref, c0, width):
        return jnp.dot(
            lhs_ref[:, :MAIN], wall[:, :, :, pl.ds(c0, width)].reshape(MAIN, width), preferred_element_type=F32
        ) + jnp.dot(lhs_ref[:, MAIN:], wrem[:, pl.ds(c0, width)], preferred_element_type=F32)

    def times_t(load, dst, j, c0, width):
        dst[j, :, :MAIN] = lax.dot_general(
            load(), wall[:, :, :, pl.ds(c0, width)].reshape(MAIN, width), NT, preferred_element_type=F32
        ).astype(BF16)
        dst[j, :, MAIN:] = lax.dot_general(
            load(), wrem[:, pl.ds(c0, width)], NT, preferred_element_type=F32
        ).astype(BF16)

    def col_copy(own, got, j, base):
        return rdma(own.at[j], got.at[j], col_send.at[base + j], col_recv.at[base + j], col_dev)

    def pass_copy(j):
        return rdma(y.at[j], x.at[j], pass_send.at[j], pass_recv.at[j], sec_dev)

    def half_copy(j):
        part_rows = pl.ds((1 - col) * 128, 128)
        return rdma(
            pm_own.at[j, part_rows], pm_got.at[j, part_rows], col_send.at[4 + j], col_recv.at[4 + j], col_dev
        )

    def mlp_copy(j, act):
        @pl.when(sec == 0)
        def _():
            act(col_copy(pm_own, pm_got, j, 4))

        @pl.when(sec == 1)
        def _():
            act(half_copy(j))

    far_arrived(1, 1)

    @pl.when(sec == 0)
    def _():
        lat_copy().wait_recv()

    def attend_step(j):
        @pl.when(sec == 1)
        def _():
            pass_copy(j).wait_recv()

        norm_rows(lambda rows: x[j, rows, :].astype(F32), mod_ref.at[0:1], mod_ref.at[1:2])
        qs[...] = times(h, 0, HEADW).astype(BF16)
        kbuf[j] = times(h, HEADW, HEADW).astype(BF16)
        vbuf[j] = times(h, 2 * HEADW, HEADW).astype(BF16)

        def heads(p, c):
            window = pl.ds(pl.multiple_of(p * 128, 128), 256)
            q_win = qs[:, window]
            k_win = kbuf[:, :, window].reshape(1024, 256)
            v_win = vbuf[:, :, window].reshape(1024, 256)
            lane = lax.broadcasted_iota(jnp.int32, (256, 256), 1) - p * 16
            mixed = att[:, window].astype(F32)
            for e in (0, 1):
                mine = (lane >= e * HD) & (lane < (e + 1) * HD)
                scores = lax.dot_general(
                    jnp.where(mine, q_win.astype(F32), 0.0).astype(BF16), k_win, NT, preferred_element_type=F32
                ) * (1.0 / math.sqrt(HD))
                scores = jnp.where(valid_ref[...] > 0, scores, -1e30)
                weights = jnp.exp(scores - jnp.max(scores, axis=-1, keepdims=True))
                totals = jnp.sum(weights, axis=-1, keepdims=True)
                got = jnp.dot(weights.astype(BF16), v_win, preferred_element_type=F32)
                mixed = jnp.where(mine, got / totals, mixed)
            att[:, window] = mixed.astype(BF16)
            return c
        lax.fori_loop(0, 4, heads, 0, unroll=2)
        times_t(lambda: att[...], pa_own, j, COL_OUT, HEADW)
        col_copy(pa_own, pa_got, j, 0).start()

    def mlp_step(j):
        col_copy(pa_own, pa_got, j, 0).wait_recv()

        def load(rows):
            v = x[j, rows, :].astype(F32) + mod_ref[2:3] * (
                pa_own[j, rows, :].astype(F32) + pa_got[j, rows, :].astype(F32)
            )
            x1[j, rows, :] = v
            return v
        norm_rows(load, mod_ref.at[3:4], mod_ref.at[4:5])

        def body(n, c):
            u = times(h, pl.multiple_of(COL_UP + n * 768, 256), 768)
            g = 0.5 * u * (1.0 + jnp.tanh(math.sqrt(2.0 / math.pi) * (u + 0.044715 * (u * u * u))))
            hid[:, pl.ds(pl.multiple_of(n * 768, 256), 768)] = g.astype(BF16)
            return c
        lax.fori_loop(0, 3, body, 0)
        times_t(lambda: hid[...], pm_own, j, COL_DOWN, 2304)
        mlp_copy(j, lambda copy: copy.start())

    def finish(j):
        mlp_copy(j, lambda copy: copy.wait_recv())

        def settle(i):
            rows = pl.ds(pl.multiple_of(i * 64, 64), 64)
            y[j, rows, :] = (
                x1[j, rows, :]
                + mod_ref[5:6] * (pm_own[j, rows, :].astype(F32) + pm_got[j, rows, :].astype(F32))
            ).astype(BF16)

        @pl.when(sec == 0)
        def _():
            lax.fori_loop(0, 4, lambda i, c: settle(i) or c, 0)
            pass_copy(j).start()

        @pl.when(sec == 1)
        def _():
            lax.fori_loop(0, 2, lambda i, c: settle(col * 2 + i) or c, 0)
        yout[j] = lax.dot_general(
            y[j, pl.ds(col * 128, 128), :], order[...], NT, preferred_element_type=F32
        ).astype(BF16)

    def step(t, carry):
        @pl.when(t < 4)
        def _():
            attend_step(t)

        @pl.when(t == 0)
        def _():
            relay_on(2, 1)

            @pl.when(sec == 0)
            def _():
                pl.semaphore_signal(go_sem, inc=1, device_id=sec_dev, device_id_type=MESH)

        @pl.when(t == 1)
        def _():
            relay_on(3, 1)
            far_arrived(2, 1)
            far_arrived(3, 1)

        @pl.when(t > 1)
        def _():
            finish(t - 2)

        @pl.when(t > 0)
        def _():
            mlp_step(t - 1)
        return carry
    lax.fori_loop(0, 5, step, 0)
    finish(3)
    for p in range(4):
        out_ref[p] = yout[slot_ref[p]]

    cond_xh.wait_send()
    for d in (1, 2, 3):
        cond_y(d, False).wait_send()
        cond_z(d, False).wait_send()
        part_z(d).wait_send()
        part_y(d).wait_send()
    part_x.wait_send()
    mod_copy.wait_send()
    for k in pieces:
        xh_copy(k).wait_send()
        for phase in (0, 1):
            for half in (0, 1):
                for link in range(4):
                    ring_copy(k, half, phase, link, False).wait_send()

    def drain(j, c):
        col_copy(pa_own, pa_got, j, 0).wait_send()
        mlp_copy(j, lambda copy: copy.wait_send())

        @pl.when(sec == 0)
        def _():
            pass_copy(j).wait_send()
        return c
    lax.fori_loop(0, 4, drain, 0)

    @pl.when(sec == 0)
    def _():
        lat_copy().wait_send()


def run_relay(place, slot, length, cond, ada, lat, stale_k, stale_v, main, rem):
    vmem = pl.BlockSpec(memory_space=pltpu.VMEM)
    tokens = (4, 256, D)
    return pl.pallas_call(
        relay,
        out_shape=jax.ShapeDtypeStruct((4, 128, D), BF16),
        in_specs=[pl.BlockSpec(memory_space=pltpu.SMEM)] * 3 + [vmem] * 7,
        out_specs=vmem,
        scratch_shapes=[
            pltpu.VMEM((D, D), BF16),
            pltpu.VMEM((1, 1024), jnp.int32),
            pltpu.VMEM((4, 128, D), BF16),
            pltpu.VMEM((4, 128, D), BF16),
            pltpu.VMEM((4, 4, 64, 128), F32),
            pltpu.VMEM((32, 128), F32),
            pltpu.VMEM((4, 4, 2, 1, MODW), F32),
            pltpu.VMEM((3, 4, 2, 1, MODW), F32),
            pltpu.VMEM((4, 2, 1, MODW), F32),
            pltpu.VMEM((3, 2, 1, MODW), F32),
            pltpu.VMEM((2, 1, MODW), F32),
            pltpu.VMEM((1, MODW), F32),
            pltpu.VMEM((1, MODW), F32),
            pltpu.VMEM((1, MODW), F32),
            pltpu.VMEM((8, D), F32),
            pltpu.VMEM((4, 4, 64, COLS), BF16),
            pltpu.VMEM((4, 4, 32, QUARTER), BF16),
            pltpu.VMEM((128, COLS), BF16),
            pltpu.VMEM(tokens, BF16),
            pltpu.VMEM(tokens, F32),
            pltpu.VMEM((256, HEADW), BF16),
            pltpu.VMEM((4, 256, HEADW), BF16),
            pltpu.VMEM((4, 256, HEADW), BF16),
            pltpu.VMEM((256, HEADW), BF16),
            pltpu.VMEM((256, 2304), BF16),
            pltpu.VMEM((256, D), BF16),
            pltpu.VMEM(tokens, BF16),
            pltpu.VMEM(tokens, BF16),
            pltpu.VMEM(tokens, BF16),
            pltpu.VMEM(tokens, BF16),
            pltpu.VMEM(tokens, BF16),
            pltpu.SemaphoreType.DMA((7,)),
            pltpu.SemaphoreType.DMA((7,)),
            pltpu.SemaphoreType.DMA((8,)),
            pltpu.SemaphoreType.DMA((8,)),
            pltpu.SemaphoreType.REGULAR,
            pltpu.SemaphoreType.DMA((3,)),
            pltpu.SemaphoreType.DMA((4,)),
            pltpu.SemaphoreType.DMA((4,)),
            pltpu.SemaphoreType.DMA((64,)),
            pltpu.SemaphoreType.DMA((64,)),
            pltpu.SemaphoreType.DMA((8,)),
            pltpu.SemaphoreType.DMA((8,)),
            pltpu.SemaphoreType.DMA((5,)),
            pltpu.SemaphoreType.DMA((5,)),
        ],
        compiler_params=pltpu.CompilerParams(
            collective_id=0, has_side_effects=True, vmem_limit_bytes=67043328
        ),
    )(place, slot, length, cond, ada, lat, stale_k, stale_v, main, rem)


def local(
    latents,
    timesteps,
    lengths,
    patch_order,
    ada_weight,
    qkv_weight,
    out_weight,
    up_weight,
    down_weight,
    stale_keys,
    stale_values,
):
    cond = jax.nn.silu(sinusoid(timesteps)).astype(BF16).astype(F32)
    cond = jnp.pad(cond.reshape(32, 36), ((0, 0), (0, 92)))
    from_col = jnp.arange(576, dtype=jnp.int32)
    group, inner = from_col // 36, from_col % 36
    to_col = jnp.where(
        inner < 32, group * 32 + inner, 512 + 64 * lax.axis_index("col") + group * 4 + inner - 32
    )
    spread = (to_col[:, None] == jnp.arange(HEADW, dtype=jnp.int32)[None, :]).astype(BF16)
    ada = jnp.einsum("dkc,ce->dke", ada_weight[0], spread, preferred_element_type=F32).astype(BF16)
    ada = jnp.pad(ada.reshape(36, MODW), ((0, 92), (0, 0)))

    pad = lambda a, n: jnp.pad(a, ((0, 0), (0, n - a.shape[1])))
    shard = jnp.concatenate(
        [pad(qkv_weight[0, :, i], HEADW) for i in range(3)]
        + [pad(out_weight[0].T, HEADW), up_weight[0], down_weight[0].T],
        axis=1,
    )
    main = shard[:32]
    rem = shard[32:].reshape(4, 4, QUARTER).transpose(1, 0, 2).reshape(16, QUARTER)

    slot = jnp.argmax(patch_order[None, :] == jnp.arange(4, dtype=jnp.int32)[:, None], axis=1).astype(jnp.int32)
    out = run_relay(
        patch_order, slot, lengths, cond, ada, latents[0], stale_keys[0, 0], stale_values[0, 0], main, rem
    )
    return out[None, None]


def solution(mesh):
    return jax.shard_map(
        local,
        mesh=mesh,
        in_specs=(
            P("row", None, "col", None),
            P("row"),
            P("row"),
            P(),
            P("section", "row", None, "col"),
            P("section", "row", None, "col"),
            P("section", "col", "row"),
            P("section", "row", "col"),
            P("section", "col", "row"),
            P("section", "row", None, None, "col"),
            P("section", "row", None, None, "col"),
        ),
        out_specs=P("section", "row", None, "col", None),
        check_vma=False,
    )
```

```python
import math

import jax
import jax.numpy as jnp
from jax import lax
from jax.experimental import pallas as pl
from jax.experimental.pallas import tpu as pltpu
from jax.sharding import PartitionSpec as P

D = 1152
HD = 72
F32 = jnp.float32
BF16 = jnp.bfloat16

HEADW = 640
COL_OUT = 3 * HEADW
COL_UP = 4 * HEADW
COL_DOWN = COL_UP + 2304
COLS = COL_DOWN + 2304
QUARTER = COLS // 4
MODW = 6 * HEADW
CHUNKS = ((0, COL_UP), (COL_UP, COL_DOWN), (COL_DOWN, COLS))
MAIN = 1024
MESH = pl.DeviceIdType.MESH
NT = (((1,), (1,)), ((), ()))


def sinusoid(step_ids):
    half_width = D // 2
    frequency = jnp.exp(-math.log(10000.0) * jnp.arange(half_width, dtype=F32) / half_width)
    angles = step_ids.astype(F32)[:, None] * frequency[None, :]
    return jnp.concatenate([jnp.cos(angles), jnp.sin(angles)], axis=1)


def halves(chunk):
    start, stop = CHUNKS[chunk]
    middle = start + (stop - start) // 2
    return ((start, middle - start), (middle, stop - middle))


def relay(
    place_ref, length_ref, cond_ref, ada_ref, lat_ref, keys_ref, values_ref, main_ref, rem_ref, out_ref,
    order, mask_ref, stale_k, stale_v, latp, yout,
    cbuf, cmat, part, got_z, sum_z, got_y, sum_y, got_x, mod_own, mod_got, mod_ref,
    wall, stag, wrem, x, x1, qs, kbuf, vbuf, att, hid, h, pa_own, pa_got, pm_own, pm_got, y,
    cond_send, cond_recv, sum_send, sum_recv, go_sem, local_sem, xh_send, xh_recv, send_sem, recv_sem, col_send, col_recv, pass_send, pass_recv,
):
    sec = lax.axis_index("section")
    row = lax.axis_index("row")
    col = lax.axis_index("col")
    z, yy, xh = row // 8, lax.rem(row // 2, 4), lax.rem(row, 2)

    def at(section=None, zz=None, y_=None, x_=None, c=None):
        s_ = sec if section is None else section
        r_ = ((z if zz is None else zz) * 4 + (yy if y_ is None else y_)) * 2 + (xh if x_ is None else x_)
        return (s_, r_, col if c is None else c)

    y_peer = [lax.rem(yy + d, 4) for d in range(4)]
    z_peer = [lax.rem(z + d, 4) for d in range(4)]
    xh_dev = at(x_=1 - xh)
    col_dev = at(c=1 - col)
    sec_dev = at(section=1 - sec)

    barrier = pltpu.get_barrier_semaphore()
    for dev in (
        [xh_dev, col_dev, sec_dev]
        + [at(y_=y_peer[d]) for d in (1, 2, 3)]
        + [at(zz=z_peer[d]) for d in (1, 2, 3)]
    ):
        pl.semaphore_signal(barrier, inc=1, device_id=dev, device_id_type=MESH)
    pl.semaphore_wait(barrier, 9)

    def rdma(src, dst, s_sem, r_sem, dev):
        return pltpu.make_async_remote_copy(
            src_ref=src, dst_ref=dst, send_sem=s_sem, recv_sem=r_sem, device_id=dev, device_id_type=MESH
        )

    def buf(k):
        return (stag, 16, rem_ref) if k == 0 else (wall, 32, main_ref)

    def span(k, half):
        if k == 0:
            return ((0, QUARTER // 2), (QUARTER // 2, QUARTER // 2))[half]
        return halves(k - 1)[half]

    pieces = range(1 + len(CHUNKS))

    def xh_copy(k):
        ref, rows, src = buf(k)
        c0 = span(k, 0)[0]
        width = span(k, 0)[1] + span(k, 1)[1]
        return rdma(
            src.at[:, pl.ds(c0, width)],
            ref.at[z, yy, pl.ds(xh * rows, rows), pl.ds(c0, width)],
            xh_send.at[k], xh_recv.at[k], xh_dev,
        )

    def xh_arrival(k):
        ref, rows, src = buf(k)
        c0 = span(k, 0)[0]
        width = span(k, 0)[1] + span(k, 1)[1]
        return rdma(
            src.at[:, pl.ds(c0, width)],
            ref.at[z, yy, pl.ds((1 - xh) * rows, rows), pl.ds(c0, width)],
            xh_send.at[k], xh_recv.at[k], xh_dev,
        )

    def ring_copy(k, half, phase, link, arrival):
        i = ((phase * 2 + half) * 4 + k) * 4 + link
        along_y = (half == 0) == (phase == 0)
        ahead = link % 2 == 0
        peers = y_peer if along_y else z_peer
        dev = at(y_=peers[1 if ahead else 3]) if along_y else at(zz=peers[1 if ahead else 3])
        if arrival:
            member = peers[(3 if ahead else 1) if link < 2 else 2]
        else:
            member = peers[0 if link < 2 else (3 if ahead else 1)]
        c0, width = span(k, half)
        if link >= 2:
            first = (width // 256) * 128 if (width // 128) % 2 == 0 else (width // 256 + 1) * 128
            c0, width = (c0, first) if ahead else (c0 + first, width - first)
        ref = buf(k)[0]
        zz, y_ = (z, member) if along_y else (member, yy)
        if phase == 0:
            ref = ref.at[zz, y_, :, pl.ds(c0, width)]
        elif along_y:
            ref = ref.at[:, y_, :, pl.ds(c0, width)]
        else:
            ref = ref.at[zz, :, :, pl.ds(c0, width)]
        return rdma(ref, ref, send_sem.at[i], recv_sem.at[i], dev)

    def near(k, phase):
        for half in (0, 1):
            for link in (0, 1):
                ring_copy(k, half, phase, link, False).start()

    def relay_on(k, phase):
        for half in (0, 1):
            for link in (0, 1):
                ring_copy(k, half, phase, link, True).wait_recv()
                ring_copy(k, half, phase, link + 2, False).start()

    def far_arrived(k, phase):
        for half in (0, 1):
            for link in (2, 3):
                ring_copy(k, half, phase, link, True).wait_recv()

    def go():
        @pl.when(sec == 0)
        def _():
            pl.semaphore_signal(go_sem, inc=1, device_id=sec_dev, device_id_type=MESH)

    def await_go():
        @pl.when(sec == 1)
        def _():
            pl.semaphore_wait(go_sem, 1)

    own_keys = pltpu.make_async_copy(keys_ref, stale_k, local_sem.at[3])
    own_values = pltpu.make_async_copy(values_ref, stale_v, local_sem.at[4])
    own_main = pltpu.make_async_copy(main_ref, wall.at[z, yy, pl.ds(xh * 32, 32)], local_sem.at[0])
    own_rem = pltpu.make_async_copy(rem_ref, stag.at[z, yy, pl.ds(xh * 16, 16)], local_sem.at[1])
    own_cond = pltpu.make_async_copy(cond_ref, cbuf.at[z, yy, pl.ds(xh * 32, 32)], local_sem.at[2])
    cond_xh = rdma(cond_ref, cbuf.at[z, yy, pl.ds(xh * 32, 32)], cond_send.at[0], cond_recv.at[0], xh_dev)
    own_cond.start()
    own_main.start()
    own_rem.start()
    own_keys.start()
    own_values.start()
    await_go()
    cond_xh.start()
    for k in pieces:
        xh_copy(k).start()

    def build_order():
        lane = lax.broadcasted_iota(jnp.int32, (128, D), 1)
        rest_lane = lane - MAIN
        source = jnp.where(
            lane < MAIN, (lane >> 5) * 36 + (lane & 31), (rest_lane >> 2) * 36 + 32 + (rest_lane & 3)
        )
        for i in range(9):
            natural = lax.broadcasted_iota(jnp.int32, (128, D), 0) + i * 128
            order[i * 128:(i + 1) * 128, :] = jnp.where(natural == source, 1.0, 0.0).astype(BF16)

    x_mine = x.at[:, pl.ds(col * 128, 128)]

    def lat_copy():
        return rdma(latp, x_mine, pass_send.at[4], pass_recv.at[4], col_dev)

    own_cond.wait()
    rdma(
        cond_ref, cbuf.at[z, yy, pl.ds((1 - xh) * 32, 32)], cond_send.at[0], cond_recv.at[0], xh_dev
    ).wait_recv()

    def cond_y(d, arrival):
        ref = cbuf.at[z, y_peer[4 - d] if arrival else yy]
        return rdma(ref, ref, cond_send.at[d], cond_recv.at[d], at(y_=y_peer[d]))

    def cond_z(d, arrival):
        ref = cbuf.at[z_peer[4 - d] if arrival else z]
        return rdma(ref, ref, cond_send.at[3 + d], cond_recv.at[3 + d], at(zz=z_peer[d]))

    def part_z(d):
        return rdma(part.at[z_peer[d]], got_z.at[d - 1], sum_send.at[d - 1], sum_recv.at[d - 1], at(zz=z_peer[d]))

    def part_y(d):
        return rdma(sum_z.at[y_peer[d]], got_y.at[d - 1], sum_send.at[d + 2], sum_recv.at[d + 2], at(y_=y_peer[d]))

    for d in (1, 3, 2):
        cond_y(d, False).start()
    for d in (1, 3, 2):
        cond_y(d, True).wait_recv()
    for d in (1, 3, 2):
        cond_z(d, False).start()
    build_order()
    for d in (1, 3, 2):
        cond_z(d, True).wait_recv()
    for i in range(32):
        cmat[i:i + 1, :] = cbuf[i // 8, (i // 2) % 4, pl.ds((i % 2) * 32 + row, 1), :]
    products = jnp.dot(cmat[...].astype(BF16), ada_ref[...], preferred_element_type=F32)
    for i in range(32):
        part[i // 8, (i // 2) % 4, i % 2] = products[i:i + 1, :]
    for d in (1, 3, 2):
        part_z(d).start()

    @pl.when(sec == 0)
    def _():
        for j in range(4):
            latp[j] = jnp.dot(lat_ref[place_ref[j]], order[...], preferred_element_type=F32).astype(BF16)

    own_main.wait()
    own_rem.wait()
    await_go()
    for k in pieces:
        xh_arrival(k).wait_recv()
        near(k, 0)
    go()

    @pl.when(sec == 0)
    def _():
        lat_copy().start()
        x[:, pl.ds(col * 128, 128), :] = latp[...]

    for d in (1, 3, 2):
        part_z(d).wait_recv()
    sum_z[...] = part[z] + got_z[0] + got_z[1] + got_z[2]
    for d in (1, 3, 2):
        part_y(d).start()
    for k in pieces:
        relay_on(k, 0)
    for d in (1, 3, 2):
        part_y(d).wait_recv()
    sum_y[...] = sum_z[yy] + got_y[0] + got_y[1] + got_y[2]
    part_x = rdma(sum_y.at[1 - xh], got_x, sum_send.at[6], sum_recv.at[6], xh_dev)
    part_x.start()
    await_go()
    far_arrived(0, 0)
    near(0, 1)
    far_arrived(1, 0)
    near(1, 1)
    part_x.wait_recv()
    mod_own[...] = sum_y[xh] + got_x[...]
    mod_copy = rdma(mod_own, mod_got, sum_send.at[7], sum_recv.at[7], col_dev)
    mod_copy.start()
    far_arrived(2, 0)
    far_arrived(3, 0)
    relay_on(0, 1)
    near(2, 1)

    own_keys.wait()
    own_values.wait()
    for j in range(4):
        kbuf[j, :, :576] = stale_k[place_ref[j]]
        vbuf[j, :, :576] = stale_v[place_ref[j]]
        kbuf[j, :, 576:] = jnp.zeros((256, HEADW - 576), BF16)
        vbuf[j, :, 576:] = jnp.zeros((256, HEADW - 576), BF16)
        token = lax.broadcasted_iota(jnp.int32, (1, 256), 1) + place_ref[j] * 256
        mask_ref[:, j * 256:(j + 1) * 256] = jnp.where(token < length_ref[0], 0.0, -1e30)
    att[...] = jnp.zeros_like(att)

    mod_copy.wait_recv()
    for k in range(6):
        base = k * HEADW
        mod_ref[k:k + 1, pl.ds(col * 512, 512)] = mod_own[:, base:base + 512]
        mod_ref[k:k + 1, pl.ds((1 - col) * 512, 512)] = mod_got[:, base:base + 512]
        mod_ref[k:k + 1, MAIN:] = mod_own[:, base + 512:base + HEADW] + mod_got[:, base + 512:base + HEADW]

    relay_on(1, 1)
    near(3, 1)
    go()
    far_arrived(0, 1)
    rows_i = lax.broadcasted_iota(jnp.int32, (128, 512), 0)
    cols_i = lax.broadcasted_iota(jnp.int32, (128, 512), 1)
    for q in range(4):
        pick = jnp.where(
            ((cols_i >> 4) == (rows_i >> 2)) & ((cols_i & 15) == 4 * q + (rows_i & 3)), 1.0, 0.0
        ).astype(BF16)
        wrem[:, q * QUARTER:(q + 1) * QUARTER] = jnp.dot(
            pick, stag[...].reshape(512, QUARTER), preferred_element_type=F32
        ).astype(BF16)

    def norm_rows(load, shift, scale):
        def body(i, carry):
            rows = pl.ds(pl.multiple_of(i * 64, 64), 64)
            v = load(rows)
            mean = jnp.sum(v, axis=-1, keepdims=True) * (1.0 / D)
            v = v - mean
            var = jnp.sum(v * v, axis=-1, keepdims=True) * (1.0 / D)
            normed = v * lax.rsqrt(var + 1e-6)
            h[rows, :] = (normed * (1.0 + scale[...]) + shift[...]).astype(BF16)
            return carry
        lax.fori_loop(0, 4, body, 0, unroll=4)

    def times(lhs_ref, c0, width):
        return jnp.dot(
            lhs_ref[:, :MAIN], wall[:, :, :, pl.ds(c0, width)].reshape(MAIN, width), preferred_element_type=F32
        ) + jnp.dot(lhs_ref[:, MAIN:], wrem[:, pl.ds(c0, width)], preferred_element_type=F32)

    def times_t(load, dst, j, c0, width):
        dst[j, :, :MAIN] = lax.dot_general(
            load(), wall[:, :, :, pl.ds(c0, width)].reshape(MAIN, width), NT, preferred_element_type=F32
        ).astype(BF16)
        dst[j, :, MAIN:] = lax.dot_general(
            load(), wrem[:, pl.ds(c0, width)], NT, preferred_element_type=F32
        ).astype(BF16)

    def col_copy(own, got, j, base):
        return rdma(own.at[j], got.at[j], col_send.at[base + j], col_recv.at[base + j], col_dev)

    def pass_copy(j):
        return rdma(y.at[j], x.at[j], pass_send.at[j], pass_recv.at[j], sec_dev)

    def half_copy(j):
        part_rows = pl.ds((1 - col) * 128, 128)
        return rdma(
            pm_own.at[j, part_rows], pm_got.at[j, part_rows], col_send.at[4 + j], col_recv.at[4 + j], col_dev
        )

    def mlp_copy(j, act):
        @pl.when(sec == 0)
        def _():
            act(col_copy(pm_own, pm_got, j, 4))

        @pl.when(sec == 1)
        def _():
            act(half_copy(j))

    far_arrived(1, 1)

    @pl.when(sec == 0)
    def _():
        lat_copy().wait_recv()

    def attend_step(j):
        @pl.when(sec == 1)
        def _():
            pass_copy(j).wait_recv()

        norm_rows(lambda rows: x[j, rows, :].astype(F32), mod_ref.at[0:1], mod_ref.at[1:2])
        qkv = times(h, 0, 3 * HEADW).astype(BF16)
        qs[...] = qkv[:, :HEADW]
        kbuf[j] = qkv[:, HEADW:2 * HEADW]
        vbuf[j] = qkv[:, 2 * HEADW:]

        def heads(p, c):
            window = pl.ds(pl.multiple_of(p * 128, 128), 256)
            q_win = qs[:, window]
            k_win = kbuf[:, :, window].reshape(1024, 256)
            v_win = vbuf[:, :, window].reshape(1024, 256)
            lane = lax.broadcasted_iota(jnp.int32, (256, 256), 1) - p * 16
            mixed = att[:, window].astype(F32)
            for e in (0, 1):
                mine = (lane >= e * HD) & (lane < (e + 1) * HD)
                scores = lax.dot_general(
                    jnp.where(mine, q_win.astype(F32), 0.0).astype(BF16), k_win, NT, preferred_element_type=F32
                ) * (math.log2(math.e) / math.sqrt(HD)) + mask_ref[...]
                weights = jnp.exp2(scores - jnp.max(scores, axis=-1, keepdims=True))
                totals = jnp.sum(weights, axis=-1, keepdims=True)
                got = jnp.dot(weights.astype(BF16), v_win, preferred_element_type=F32)
                mixed = jnp.where(mine, got * (1.0 / totals), mixed)
            att[:, window] = mixed.astype(BF16)
            return c
        lax.fori_loop(0, 4, heads, 0, unroll=4)
        times_t(lambda: att[...], pa_own, j, COL_OUT, HEADW)
        col_copy(pa_own, pa_got, j, 0).start()

    def mlp_step(j):
        col_copy(pa_own, pa_got, j, 0).wait_recv()

        def load(rows):
            v = x[j, rows, :].astype(F32) + mod_ref[2:3] * (
                pa_own[j, rows, :].astype(F32) + pa_got[j, rows, :].astype(F32)
            )
            x1[j, rows, :] = v
            return v
        norm_rows(load, mod_ref.at[3:4], mod_ref.at[4:5])

        def body(n, c):
            u = times(h, pl.multiple_of(COL_UP + n * 768, 256), 768)
            g = 0.5 * u * (1.0 + jnp.tanh(math.sqrt(2.0 / math.pi) * (u + 0.044715 * (u * u * u))))
            hid[:, pl.ds(pl.multiple_of(n * 768, 256), 768)] = g.astype(BF16)
            return c
        lax.fori_loop(0, 3, body, 0, unroll=3)
        times_t(lambda: hid[...], pm_own, j, COL_DOWN, 2304)
        mlp_copy(j, lambda copy: copy.start())

    def finish(j):
        mlp_copy(j, lambda copy: copy.wait_recv())

        def settle(i):
            rows = pl.ds(pl.multiple_of(i * 64, 64), 64)
            y[j, rows, :] = (
                x1[j, rows, :]
                + mod_ref[5:6] * (pm_own[j, rows, :].astype(F32) + pm_got[j, rows, :].astype(F32))
            ).astype(BF16)

        @pl.when(sec == 0)
        def _():
            lax.fori_loop(0, 4, lambda i, c: settle(i) or c, 0)
            pass_copy(j).start()

        @pl.when(sec == 1)
        def _():
            lax.fori_loop(0, 2, lambda i, c: settle(col * 2 + i) or c, 0)
        yout[j] = lax.dot_general(
            y[j, pl.ds(col * 128, 128), :], order[...], NT, preferred_element_type=F32
        ).astype(BF16)

    def step(t, carry):
        @pl.when(t < 4)
        def _():
            attend_step(t)

        @pl.when(t == 0)
        def _():
            relay_on(2, 1)
            relay_on(3, 1)
            go()

        @pl.when(t == 1)
        def _():
            far_arrived(2, 1)
            far_arrived(3, 1)

        @pl.when(t > 1)
        def _():
            finish(t - 2)

        @pl.when(t > 0)
        def _():
            mlp_step(t - 1)
        return carry
    lax.fori_loop(0, 5, step, 0)
    finish(3)
    for p in range(4):
        slot = jnp.int32(0)
        for j in range(1, 4):
            slot = jnp.where(place_ref[j] == p, j, slot)
        out_ref[p] = yout[slot]

    cond_xh.wait_send()
    for d in (1, 2, 3):
        cond_y(d, False).wait_send()
        cond_z(d, False).wait_send()
        part_z(d).wait_send()
        part_y(d).wait_send()
    part_x.wait_send()
    mod_copy.wait_send()
    for k in pieces:
        xh_copy(k).wait_send()
        for phase in (0, 1):
            for half in (0, 1):
                for link in range(4):
                    ring_copy(k, half, phase, link, False).wait_send()

    def drain(j, c):
        col_copy(pa_own, pa_got, j, 0).wait_send()
        mlp_copy(j, lambda copy: copy.wait_send())

        @pl.when(sec == 0)
        def _():
            pass_copy(j).wait_send()
        return c
    lax.fori_loop(0, 4, drain, 0)

    @pl.when(sec == 0)
    def _():
        lat_copy().wait_send()


def run_relay(place, length, cond, ada, lat, stale_k, stale_v, main, rem):
    vmem = pl.BlockSpec(memory_space=pltpu.VMEM)
    tokens = (4, 256, D)
    return pl.pallas_call(
        relay,
        out_shape=jax.ShapeDtypeStruct((4, 128, D), BF16),
        in_specs=[pl.BlockSpec(memory_space=pltpu.SMEM)] * 2 + [vmem] * 3 + [pl.BlockSpec(memory_space=pl.ANY)] * 2 + [vmem] * 2,
        out_specs=vmem,
        scratch_shapes=[
            pltpu.VMEM((D, D), BF16),
            pltpu.VMEM((1, 1024), F32),
            pltpu.VMEM((4, 256, 576), BF16),
            pltpu.VMEM((4, 256, 576), BF16),
            pltpu.VMEM((4, 128, D), BF16),
            pltpu.VMEM((4, 128, D), BF16),
            pltpu.VMEM((4, 4, 64, 128), F32),
            pltpu.VMEM((32, 128), F32),
            pltpu.VMEM((4, 4, 2, 1, MODW), F32),
            pltpu.VMEM((3, 4, 2, 1, MODW), F32),
            pltpu.VMEM((4, 2, 1, MODW), F32),
            pltpu.VMEM((3, 2, 1, MODW), F32),
            pltpu.VMEM((2, 1, MODW), F32),
            pltpu.VMEM((1, MODW), F32),
            pltpu.VMEM((1, MODW), F32),
            pltpu.VMEM((1, MODW), F32),
            pltpu.VMEM((8, D), F32),
            pltpu.VMEM((4, 4, 64, COLS), BF16),
            pltpu.VMEM((4, 4, 32, QUARTER), BF16),
            pltpu.VMEM((128, COLS), BF16),
            pltpu.VMEM(tokens, BF16),
            pltpu.VMEM(tokens, F32),
            pltpu.VMEM((256, HEADW), BF16),
            pltpu.VMEM((4, 256, HEADW), BF16),
            pltpu.VMEM((4, 256, HEADW), BF16),
            pltpu.VMEM((256, HEADW), BF16),
            pltpu.VMEM((256, 2304), BF16),
            pltpu.VMEM((256, D), BF16),
            pltpu.VMEM(tokens, BF16),
            pltpu.VMEM(tokens, BF16),
            pltpu.VMEM(tokens, BF16),
            pltpu.VMEM(tokens, BF16),
            pltpu.VMEM(tokens, BF16),
            pltpu.SemaphoreType.DMA((7,)),
            pltpu.SemaphoreType.DMA((7,)),
            pltpu.SemaphoreType.DMA((8,)),
            pltpu.SemaphoreType.DMA((8,)),
            pltpu.SemaphoreType.REGULAR,
            pltpu.SemaphoreType.DMA((5,)),
            pltpu.SemaphoreType.DMA((4,)),
            pltpu.SemaphoreType.DMA((4,)),
            pltpu.SemaphoreType.DMA((64,)),
            pltpu.SemaphoreType.DMA((64,)),
            pltpu.SemaphoreType.DMA((8,)),
            pltpu.SemaphoreType.DMA((8,)),
            pltpu.SemaphoreType.DMA((5,)),
            pltpu.SemaphoreType.DMA((5,)),
        ],
        compiler_params=pltpu.CompilerParams(
            collective_id=0, has_side_effects=True, vmem_limit_bytes=67043328
        ),
    )(place, length, cond, ada, lat, stale_k, stale_v, main, rem)


def local(
    latents,
    timesteps,
    lengths,
    patch_order,
    ada_weight,
    qkv_weight,
    out_weight,
    up_weight,
    down_weight,
    stale_keys,
    stale_values,
):
    cond = jax.nn.silu(sinusoid(timesteps)).astype(BF16).astype(F32)
    cond = jnp.pad(cond.reshape(32, 36), ((0, 0), (0, 92)))
    from_col = jnp.arange(576, dtype=jnp.int32)
    group, inner = from_col // 36, from_col % 36
    to_col = jnp.where(
        inner < 32, group * 32 + inner, 512 + 64 * lax.axis_index("col") + group * 4 + inner - 32
    )
    spread = (to_col[:, None] == jnp.arange(HEADW, dtype=jnp.int32)[None, :]).astype(BF16)
    ada = jnp.einsum("dkc,ce->dke", ada_weight[0], spread, preferred_element_type=F32).astype(BF16)
    ada = jnp.pad(ada.reshape(36, MODW), ((0, 92), (0, 0)))

    pad = lambda a, n: jnp.pad(a, ((0, 0), (0, n - a.shape[1])))
    shard = jnp.concatenate(
        [pad(qkv_weight[0, :, i], HEADW) for i in range(3)]
        + [pad(out_weight[0].T, HEADW), up_weight[0], down_weight[0].T],
        axis=1,
    )
    main = shard[:32]
    rem = shard[32:].reshape(4, 4, QUARTER).transpose(1, 0, 2).reshape(16, QUARTER)

    out = run_relay(
        patch_order, lengths, cond, ada, latents[0], stale_keys[0, 0], stale_values[0, 0], main, rem
    )
    return out[None, None]


def solution(mesh):
    return jax.shard_map(
        local,
        mesh=mesh,
        in_specs=(
            P("row", None, "col", None),
            P("row"),
            P("row"),
            P(),
            P("section", "row", None, "col"),
            P("section", "row", None, "col"),
            P("section", "col", "row"),
            P("section", "row", "col"),
            P("section", "col", "row"),
            P("section", "row", None, None, "col"),
            P("section", "row", None, None, "col"),
        ),
        out_specs=P("section", "row", None, "col", None),
        check_vma=False,
    )
```

```python
import math

import jax
import jax.numpy as jnp
from jax import lax
from jax.experimental import pallas as pl
from jax.experimental.pallas import tpu as pltpu
from jax.sharding import PartitionSpec as P

D = 1152
HD = 72
F32 = jnp.float32
BF16 = jnp.bfloat16

HEADW = 640
COL_OUT = 3 * HEADW
COL_UP = 4 * HEADW
COL_DOWN = COL_UP + 2304
COLS = COL_DOWN + 2304
QUARTER = COLS // 4
MODW = 6 * HEADW
ADAROWS = 48
CHUNKS = ((0, COL_UP), (COL_UP, COL_DOWN), (COL_DOWN, COLS))
MAIN = 1024
MESH = pl.DeviceIdType.MESH
NT = (((1,), (1,)), ((), ()))


def sinusoid(step_ids):
    half_width = D // 2
    frequency = jnp.exp(-math.log(10000.0) * jnp.arange(half_width, dtype=F32) / half_width)
    angles = step_ids.astype(F32)[:, None] * frequency[None, :]
    return jnp.concatenate([jnp.cos(angles), jnp.sin(angles)], axis=1)


def halves(chunk):
    start, stop = CHUNKS[chunk]
    middle = start + (stop - start) // 2
    return ((start, middle - start), (middle, stop - middle))


def relay(
    place_ref, length_ref, cond_ref, ada_ref, lat_ref, keys_ref, values_ref, main_ref, rem_ref, out_ref,
    order, mask_ref, stale_k, stale_v, latp, yout,
    cbuf, cmat, ada_got, part, got_z, sum_z, got_y, sum_y, got_x, mods, mod_ref,
    wall, stag, wrem, x, x1, qs, kbuf, vbuf, att, hid, h, pa_own, pa_got, pm_own, pm_got, y,
    give_send, give_recv, cond_send, cond_recv, sum_send, sum_recv, go_sem, local_sem, xh_send, xh_recv, send_sem, recv_sem, col_send, col_recv, pass_send, pass_recv,
):
    sec = lax.axis_index("section")
    row = lax.axis_index("row")
    col = lax.axis_index("col")
    z, yy, xh = row // 8, lax.rem(row // 2, 4), lax.rem(row, 2)

    def at(section=None, zz=None, y_=None, x_=None, c=None):
        s_ = sec if section is None else section
        r_ = ((z if zz is None else zz) * 4 + (yy if y_ is None else y_)) * 2 + (xh if x_ is None else x_)
        return (s_, r_, col if c is None else c)

    y_peer = [lax.rem(yy + d, 4) for d in range(4)]
    z_peer = [lax.rem(z + d, 4) for d in range(4)]
    xh_dev = at(x_=1 - xh)
    col_dev = at(c=1 - col)
    sec_dev = at(section=1 - sec)

    barrier = pltpu.get_barrier_semaphore()
    for dev in (
        [xh_dev, col_dev, sec_dev]
        + [at(y_=y_peer[d]) for d in (1, 2, 3)]
        + [at(zz=z_peer[d]) for d in (1, 2, 3)]
    ):
        pl.semaphore_signal(barrier, inc=1, device_id=dev, device_id_type=MESH)
    pl.semaphore_wait(barrier, 9)

    def rdma(src, dst, s_sem, r_sem, dev):
        return pltpu.make_async_remote_copy(
            src_ref=src, dst_ref=dst, send_sem=s_sem, recv_sem=r_sem, device_id=dev, device_id_type=MESH
        )

    def buf(k):
        return (stag, 16, rem_ref) if k == 0 else (wall, 32, main_ref)

    def span(k, half):
        if k == 0:
            return ((0, QUARTER // 2), (QUARTER // 2, QUARTER // 2))[half]
        return halves(k - 1)[half]

    pieces = range(1 + len(CHUNKS))

    def xh_copy(k):
        ref, rows, src = buf(k)
        c0 = span(k, 0)[0]
        width = span(k, 0)[1] + span(k, 1)[1]
        return rdma(
            src.at[:, pl.ds(c0, width)],
            ref.at[z, yy, pl.ds(xh * rows, rows), pl.ds(c0, width)],
            xh_send.at[k], xh_recv.at[k], xh_dev,
        )

    def xh_arrival(k):
        ref, rows, src = buf(k)
        c0 = span(k, 0)[0]
        width = span(k, 0)[1] + span(k, 1)[1]
        return rdma(
            src.at[:, pl.ds(c0, width)],
            ref.at[z, yy, pl.ds((1 - xh) * rows, rows), pl.ds(c0, width)],
            xh_send.at[k], xh_recv.at[k], xh_dev,
        )

    def ring_copy(k, half, phase, link, arrival):
        i = ((phase * 2 + half) * 4 + k) * 4 + link
        along_y = (half == 0) == (phase == 0)
        ahead = link % 2 == 0
        peers = y_peer if along_y else z_peer
        dev = at(y_=peers[1 if ahead else 3]) if along_y else at(zz=peers[1 if ahead else 3])
        if arrival:
            member = peers[(3 if ahead else 1) if link < 2 else 2]
        else:
            member = peers[0 if link < 2 else (3 if ahead else 1)]
        c0, width = span(k, half)
        if link >= 2:
            first = (width // 256) * 128 if (width // 128) % 2 == 0 else (width // 256 + 1) * 128
            c0, width = (c0, first) if ahead else (c0 + first, width - first)
        ref = buf(k)[0]
        zz, y_ = (z, member) if along_y else (member, yy)
        if phase == 0:
            ref = ref.at[zz, y_, :, pl.ds(c0, width)]
        elif along_y:
            ref = ref.at[:, y_, :, pl.ds(c0, width)]
        else:
            ref = ref.at[zz, :, :, pl.ds(c0, width)]
        return rdma(ref, ref, send_sem.at[i], recv_sem.at[i], dev)

    def near(k, phase):
        for half in (0, 1):
            for link in (0, 1):
                ring_copy(k, half, phase, link, False).start()

    def relay_on(k, phase):
        for half in (0, 1):
            for link in (0, 1):
                ring_copy(k, half, phase, link, True).wait_recv()
                ring_copy(k, half, phase, link + 2, False).start()

    def far_arrived(k, phase):
        for half in (0, 1):
            for link in (2, 3):
                ring_copy(k, half, phase, link, True).wait_recv()

    def go():
        @pl.when(sec == 0)
        def _():
            pl.semaphore_signal(go_sem, inc=1, device_id=sec_dev, device_id_type=MESH)

    def await_go():
        @pl.when(sec == 1)
        def _():
            pl.semaphore_wait(go_sem, 1)

    own_keys = pltpu.make_async_copy(keys_ref, stale_k, local_sem.at[3])
    own_values = pltpu.make_async_copy(values_ref, stale_v, local_sem.at[4])
    own_main = pltpu.make_async_copy(main_ref, wall.at[z, yy, pl.ds(xh * 32, 32)], local_sem.at[0])
    own_rem = pltpu.make_async_copy(rem_ref, stag.at[z, yy, pl.ds(xh * 16, 16)], local_sem.at[1])
    own_cond = pltpu.make_async_copy(cond_ref, cbuf.at[z, yy, pl.ds(xh * 32, 32)], local_sem.at[2])
    cond_xh = rdma(cond_ref, cbuf.at[z, yy, pl.ds(xh * 32, 32)], cond_send.at[0], cond_recv.at[0], xh_dev)
    own_main.start()
    own_rem.start()
    own_keys.start()
    own_values.start()
    ada_copy = rdma(ada_ref, ada_got, give_send.at[0], give_recv.at[0], sec_dev)
    mods_0 = mods.at[:, :, pl.ds(0, MODW)]
    mods_copy = rdma(mods_0, mods_0, give_send.at[1], give_recv.at[1], sec_dev)

    @pl.when(sec == 0)
    def _():
        ada_copy.start()

    def build_order():
        lane = lax.broadcasted_iota(jnp.int32, (128, D), 1)
        rest_lane = lane - MAIN
        source = jnp.where(
            lane < MAIN, (lane >> 5) * 36 + (lane & 31), (rest_lane >> 2) * 36 + 32 + (rest_lane & 3)
        )
        for i in range(9):
            natural = lax.broadcasted_iota(jnp.int32, (128, D), 0) + i * 128
            order[i * 128:(i + 1) * 128, :] = jnp.where(natural == source, 1.0, 0.0).astype(BF16)

    def lat_copy(j):
        return rdma(
            latp.at[j], x.at[j, pl.ds(col * 128, 128)], pass_send.at[4 + j], pass_recv.at[4 + j], col_dev
        )

    def send_piece(k):
        xh_arrival(k).wait_recv()
        near(k, 0)

    def cond_y(d, arrival):
        ref = cbuf.at[z, y_peer[4 - d] if arrival else yy]
        return rdma(ref, ref, cond_send.at[d], cond_recv.at[d], at(y_=y_peer[d]))

    def cond_z(d, arrival):
        ref = cbuf.at[z_peer[4 - d] if arrival else z]
        return rdma(ref, ref, cond_send.at[3 + d], cond_recv.at[3 + d], at(zz=z_peer[d]))

    def part_z(d):
        return rdma(part.at[z_peer[d]], got_z.at[d - 1], sum_send.at[d - 1], sum_recv.at[d - 1], at(zz=z_peer[d]))

    def part_y(d):
        return rdma(sum_z.at[y_peer[d]], got_y.at[d - 1], sum_send.at[d + 2], sum_recv.at[d + 2], at(y_=y_peer[d]))

    part_x = rdma(sum_y.at[1 - xh], got_x, sum_send.at[6], sum_recv.at[6], xh_dev)
    mod_copy = rdma(mods.at[col], mods.at[col], sum_send.at[7], sum_recv.at[7], col_dev)

    @pl.when(sec == 1)
    def _():
        own_cond.start()
        cond_xh.start()
        own_cond.wait()
        rdma(
            cond_ref, cbuf.at[z, yy, pl.ds((1 - xh) * 32, 32)], cond_send.at[0], cond_recv.at[0], xh_dev
        ).wait_recv()
        for d in (1, 3, 2):
            cond_y(d, False).start()
        for d in (1, 3, 2):
            cond_y(d, True).wait_recv()
        for d in (1, 3, 2):
            cond_z(d, False).start()
        for d in (1, 3, 2):
            cond_z(d, True).wait_recv()
        for i in range(32):
            cmat[i:i + 1, :] = cbuf[i // 8, (i // 2) % 4, pl.ds((i % 2) * 32 + row, 1), :]
        ada_copy.wait_recv()
        for n, weight in ((0, ada_got), (1, ada_ref)):
            products = jnp.dot(
                cmat[:, :ADAROWS].astype(BF16), weight[...], preferred_element_type=F32
            )
            for i in range(32):
                part[i // 8, (i // 2) % 4, i % 2, :, n * MODW:(n + 1) * MODW] = products[i:i + 1, :]
        for d in (1, 3, 2):
            part_z(d).start()
        for d in (1, 3, 2):
            part_z(d).wait_recv()
        sum_z[...] = part[z] + got_z[0] + got_z[1] + got_z[2]
        for d in (1, 3, 2):
            part_y(d).start()
        for d in (1, 3, 2):
            part_y(d).wait_recv()
        sum_y[...] = sum_z[yy] + got_y[0] + got_y[1] + got_y[2]
        part_x.start()
        part_x.wait_recv()
        mods[col] = sum_y[xh] + got_x[...]
        mod_copy.start()
        rdma(
            mods.at[1 - col], mods.at[1 - col], sum_send.at[7], sum_recv.at[7], col_dev
        ).wait_recv()
        mods_copy.start()

    await_go()
    for k in pieces:
        xh_copy(k).start()
    own_main.wait()
    own_rem.wait()
    await_go()
    for k in pieces:
        send_piece(k)
    go()
    for k in pieces:
        relay_on(k, 0)
    await_go()
    far_arrived(0, 0)
    near(0, 1)
    far_arrived(1, 0)
    near(1, 1)
    build_order()

    @pl.when(sec == 0)
    def _():
        for j in range(4):
            latp[j] = jnp.dot(lat_ref[place_ref[j]], order[...], preferred_element_type=F32).astype(BF16)
        for j in range(4):
            lat_copy(j).start()
        x[:, pl.ds(col * 128, 128), :] = latp[...]

    far_arrived(2, 0)
    far_arrived(3, 0)
    relay_on(0, 1)
    near(2, 1)

    own_keys.wait()
    own_values.wait()
    for j in range(4):
        kbuf[j, :, :576] = stale_k[place_ref[j]]
        vbuf[j, :, :576] = stale_v[place_ref[j]]
        kbuf[j, :, 576:] = jnp.zeros((256, HEADW - 576), BF16)
        vbuf[j, :, 576:] = jnp.zeros((256, HEADW - 576), BF16)
        token = lax.broadcasted_iota(jnp.int32, (1, 256), 1) + place_ref[j] * 256
        mask_ref[:, j * 256:(j + 1) * 256] = jnp.where(token < length_ref[0], 0.0, -1e30)
    att[...] = jnp.zeros_like(att)

    relay_on(1, 1)
    near(3, 1)
    go()
    far_arrived(0, 1)
    rows_i = lax.broadcasted_iota(jnp.int32, (128, 512), 0)
    cols_i = lax.broadcasted_iota(jnp.int32, (128, 512), 1)
    for q in range(4):
        pick = jnp.where(
            ((cols_i >> 4) == (rows_i >> 2)) & ((cols_i & 15) == 4 * q + (rows_i & 3)), 1.0, 0.0
        ).astype(BF16)
        wrem[:, q * QUARTER:(q + 1) * QUARTER] = jnp.dot(
            pick, stag[...].reshape(512, QUARTER), preferred_element_type=F32
        ).astype(BF16)

    def norm_rows(load, shift, scale):
        def body(i, carry):
            rows = pl.ds(pl.multiple_of(i * 64, 64), 64)
            v = load(rows)
            mean = jnp.sum(v, axis=-1, keepdims=True) * (1.0 / D)
            v = v - mean
            var = jnp.sum(v * v, axis=-1, keepdims=True) * (1.0 / D)
            normed = v * lax.rsqrt(var + 1e-6)
            h[rows, :] = (normed * (1.0 + scale[...]) + shift[...]).astype(BF16)
            return carry
        lax.fori_loop(0, 4, body, 0, unroll=4)

    def times(lhs_ref, c0, width):
        return jnp.dot(
            lhs_ref[:, :MAIN], wall[:, :, :, pl.ds(c0, width)].reshape(MAIN, width), preferred_element_type=F32
        ) + jnp.dot(lhs_ref[:, MAIN:], wrem[:, pl.ds(c0, width)], preferred_element_type=F32)

    def times_t(load, dst, j, c0, width):
        dst[j, :, :MAIN] = lax.dot_general(
            load(), wall[:, :, :, pl.ds(c0, width)].reshape(MAIN, width), NT, preferred_element_type=F32
        ).astype(BF16)
        dst[j, :, MAIN:] = lax.dot_general(
            load(), wrem[:, pl.ds(c0, width)], NT, preferred_element_type=F32
        ).astype(BF16)

    def col_copy(own, got, j, base):
        return rdma(own.at[j], got.at[j], col_send.at[base + j], col_recv.at[base + j], col_dev)

    def pass_copy(j):
        return rdma(y.at[j], x.at[j], pass_send.at[j], pass_recv.at[j], sec_dev)

    def half_copy(j):
        part_rows = pl.ds((1 - col) * 128, 128)
        return rdma(
            pm_own.at[j, part_rows], pm_got.at[j, part_rows], col_send.at[4 + j], col_recv.at[4 + j], col_dev
        )

    def mlp_copy(j, act):
        @pl.when(sec == 0)
        def _():
            act(col_copy(pm_own, pm_got, j, 4))

        @pl.when(sec == 1)
        def _():
            act(half_copy(j))

    @pl.when(sec == 0)
    def _():
        mods_copy.wait_recv()
    for k in range(6):
        base = pl.multiple_of(sec * MODW + k * HEADW, 128)
        rest_base = pl.multiple_of(base + 512, 128)
        for c in (0, 1):
            mod_ref[k:k + 1, c * 512:(c + 1) * 512] = mods[c, :, pl.ds(base, 512)]
        mod_ref[k:k + 1, MAIN:] = mods[0, :, pl.ds(rest_base, 128)] + mods[1, :, pl.ds(rest_base, 128)]

    far_arrived(1, 1)

    def attend_step(j):
        @pl.when(sec == 0)
        def _():
            lat_copy(j).wait_recv()

        @pl.when(sec == 1)
        def _():
            pass_copy(j).wait_recv()

        norm_rows(lambda rows: x[j, rows, :].astype(F32), mod_ref.at[0:1], mod_ref.at[1:2])
        qkv = times(h, 0, 3 * HEADW).astype(BF16)
        qs[...] = qkv[:, :HEADW]
        kbuf[j] = qkv[:, HEADW:2 * HEADW]
        vbuf[j] = qkv[:, 2 * HEADW:]

        def heads(p, c):
            window = pl.ds(pl.multiple_of(p * 128, 128), 256)
            q_win = qs[:, window]
            k_win = kbuf[:, :, window].reshape(1024, 256)
            v_win = vbuf[:, :, window].reshape(1024, 256)
            lane = lax.broadcasted_iota(jnp.int32, (256, 256), 1) - p * 16
            mixed = att[:, window].astype(F32)
            for e in (0, 1):
                mine = (lane >= e * HD) & (lane < (e + 1) * HD)
                scores = lax.dot_general(
                    jnp.where(mine, q_win.astype(F32), 0.0).astype(BF16), k_win, NT, preferred_element_type=F32
                ) * (math.log2(math.e) / math.sqrt(HD)) + mask_ref[...]
                weights = jnp.exp2(scores - jnp.max(scores, axis=-1, keepdims=True))
                totals = jnp.sum(weights, axis=-1, keepdims=True)
                got = jnp.dot(weights.astype(BF16), v_win, preferred_element_type=F32)
                mixed = jnp.where(mine, got * (1.0 / totals), mixed)
            att[:, window] = mixed.astype(BF16)
            return c
        lax.fori_loop(0, 4, heads, 0, unroll=4)
        times_t(lambda: att[...], pa_own, j, COL_OUT, HEADW)
        col_copy(pa_own, pa_got, j, 0).start()

    def mlp_step(j):
        col_copy(pa_own, pa_got, j, 0).wait_recv()

        def load(rows):
            v = x[j, rows, :].astype(F32) + mod_ref[2:3] * (
                pa_own[j, rows, :].astype(F32) + pa_got[j, rows, :].astype(F32)
            )
            x1[j, rows, :] = v
            return v
        norm_rows(load, mod_ref.at[3:4], mod_ref.at[4:5])

        def body(n, c):
            u = times(h, pl.multiple_of(COL_UP + n * 768, 256), 768)
            g = 0.5 * u * (1.0 + jnp.tanh(math.sqrt(2.0 / math.pi) * (u + 0.044715 * (u * u * u))))
            hid[:, pl.ds(pl.multiple_of(n * 768, 256), 768)] = g.astype(BF16)
            return c
        lax.fori_loop(0, 3, body, 0, unroll=3)
        times_t(lambda: hid[...], pm_own, j, COL_DOWN, 2304)
        mlp_copy(j, lambda copy: copy.start())

    def finish(j):
        mlp_copy(j, lambda copy: copy.wait_recv())

        def settle(i):
            rows = pl.ds(pl.multiple_of(i * 64, 64), 64)
            y[j, rows, :] = (
                x1[j, rows, :]
                + mod_ref[5:6] * (pm_own[j, rows, :].astype(F32) + pm_got[j, rows, :].astype(F32))
            ).astype(BF16)

        @pl.when(sec == 0)
        def _():
            lax.fori_loop(0, 4, lambda i, c: settle(i) or c, 0)
            pass_copy(j).start()

        @pl.when(sec == 1)
        def _():
            lax.fori_loop(0, 2, lambda i, c: settle(col * 2 + i) or c, 0)
        yout[j] = lax.dot_general(
            y[j, pl.ds(col * 128, 128), :], order[...], NT, preferred_element_type=F32
        ).astype(BF16)

    def first_half(t, carry):
        attend_step(t)

        @pl.when(t == 0)
        def _():
            relay_on(2, 1)
            relay_on(3, 1)
            go()
        return carry
    lax.fori_loop(0, 4, first_half, 0)
    far_arrived(2, 1)
    far_arrived(3, 1)

    def second_half(t, carry):
        mlp_step(t)

        @pl.when(t > 0)
        def _():
            finish(t - 1)
        return carry
    lax.fori_loop(0, 4, second_half, 0)
    finish(3)
    for p in range(4):
        slot = jnp.int32(0)
        for j in range(1, 4):
            slot = jnp.where(place_ref[j] == p, j, slot)
        out_ref[p] = yout[slot]

    @pl.when(sec == 0)
    def _():
        ada_copy.wait_send()

    @pl.when(sec == 1)
    def _():
        cond_xh.wait_send()
        for d in (1, 2, 3):
            cond_y(d, False).wait_send()
            cond_z(d, False).wait_send()
            part_z(d).wait_send()
            part_y(d).wait_send()
        part_x.wait_send()
        mod_copy.wait_send()
        mods_copy.wait_send()

    for k in pieces:
        xh_copy(k).wait_send()
        for phase in (0, 1):
            for half in (0, 1):
                for link in range(4):
                    ring_copy(k, half, phase, link, False).wait_send()

    def drain(j, c):
        col_copy(pa_own, pa_got, j, 0).wait_send()
        mlp_copy(j, lambda copy: copy.wait_send())

        @pl.when(sec == 0)
        def _():
            pass_copy(j).wait_send()
            lat_copy(j).wait_send()
        return c
    lax.fori_loop(0, 4, drain, 0)


def run_relay(place, length, cond, ada, lat, stale_k, stale_v, main, rem):
    vmem = pl.BlockSpec(memory_space=pltpu.VMEM)
    tokens = (4, 256, D)
    return pl.pallas_call(
        relay,
        out_shape=jax.ShapeDtypeStruct((4, 128, D), BF16),
        in_specs=[pl.BlockSpec(memory_space=pltpu.SMEM)] * 2 + [vmem] * 3 + [pl.BlockSpec(memory_space=pl.ANY)] * 2 + [vmem] * 2,
        out_specs=vmem,
        scratch_shapes=[
            pltpu.VMEM((D, D), BF16),
            pltpu.VMEM((1, 1024), F32),
            pltpu.VMEM((4, 256, 576), BF16),
            pltpu.VMEM((4, 256, 576), BF16),
            pltpu.VMEM((4, 128, D), BF16),
            pltpu.VMEM((4, 128, D), BF16),
            pltpu.VMEM((4, 4, 64, 128), F32),
            pltpu.VMEM((32, 128), F32),
            pltpu.VMEM((ADAROWS, MODW), BF16),
            pltpu.VMEM((4, 4, 2, 1, 2 * MODW), F32),
            pltpu.VMEM((3, 4, 2, 1, 2 * MODW), F32),
            pltpu.VMEM((4, 2, 1, 2 * MODW), F32),
            pltpu.VMEM((3, 2, 1, 2 * MODW), F32),
            pltpu.VMEM((2, 1, 2 * MODW), F32),
            pltpu.VMEM((1, 2 * MODW), F32),
            pltpu.VMEM((2, 1, 2 * MODW), F32),
            pltpu.VMEM((8, D), F32),
            pltpu.VMEM((4, 4, 64, COLS), BF16),
            pltpu.VMEM((4, 4, 32, QUARTER), BF16),
            pltpu.VMEM((128, COLS), BF16),
            pltpu.VMEM(tokens, BF16),
            pltpu.VMEM(tokens, F32),
            pltpu.VMEM((256, HEADW), BF16),
            pltpu.VMEM((4, 256, HEADW), BF16),
            pltpu.VMEM((4, 256, HEADW), BF16),
            pltpu.VMEM((256, HEADW), BF16),
            pltpu.VMEM((256, 2304), BF16),
            pltpu.VMEM((256, D), BF16),
            pltpu.VMEM(tokens, BF16),
            pltpu.VMEM(tokens, BF16),
            pltpu.VMEM(tokens, BF16),
            pltpu.VMEM(tokens, BF16),
            pltpu.VMEM(tokens, BF16),
            pltpu.SemaphoreType.DMA((2,)),
            pltpu.SemaphoreType.DMA((2,)),
            pltpu.SemaphoreType.DMA((7,)),
            pltpu.SemaphoreType.DMA((7,)),
            pltpu.SemaphoreType.DMA((8,)),
            pltpu.SemaphoreType.DMA((8,)),
            pltpu.SemaphoreType.REGULAR,
            pltpu.SemaphoreType.DMA((5,)),
            pltpu.SemaphoreType.DMA((4,)),
            pltpu.SemaphoreType.DMA((4,)),
            pltpu.SemaphoreType.DMA((64,)),
            pltpu.SemaphoreType.DMA((64,)),
            pltpu.SemaphoreType.DMA((8,)),
            pltpu.SemaphoreType.DMA((8,)),
            pltpu.SemaphoreType.DMA((8,)),
            pltpu.SemaphoreType.DMA((8,)),
        ],
        compiler_params=pltpu.CompilerParams(
            collective_id=0, has_side_effects=True, vmem_limit_bytes=67043328
        ),
    )(place, length, cond, ada, lat, stale_k, stale_v, main, rem)


def local(
    latents,
    timesteps,
    lengths,
    patch_order,
    ada_weight,
    qkv_weight,
    out_weight,
    up_weight,
    down_weight,
    stale_keys,
    stale_values,
):
    cond = jax.nn.silu(sinusoid(timesteps)).astype(BF16).astype(F32)
    cond = jnp.pad(cond.reshape(32, 36), ((0, 0), (0, 92)))
    from_col = jnp.arange(576, dtype=jnp.int32)
    group, inner = from_col // 36, from_col % 36
    to_col = jnp.where(
        inner < 32, group * 32 + inner, 512 + 64 * lax.axis_index("col") + group * 4 + inner - 32
    )
    spread = (to_col[:, None] == jnp.arange(HEADW, dtype=jnp.int32)[None, :]).astype(BF16)
    ada = jnp.einsum("dkc,ce->dke", ada_weight[0], spread, preferred_element_type=F32).astype(BF16)
    ada = jnp.pad(ada.reshape(36, MODW), ((0, ADAROWS - 36), (0, 0)))

    pad = lambda a, n: jnp.pad(a, ((0, 0), (0, n - a.shape[1])))
    shard = jnp.concatenate(
        [pad(qkv_weight[0, :, i], HEADW) for i in range(3)]
        + [pad(out_weight[0].T, HEADW), up_weight[0], down_weight[0].T],
        axis=1,
    )
    main = shard[:32]
    rem = shard[32:].reshape(4, 4, QUARTER).transpose(1, 0, 2).reshape(16, QUARTER)

    out = run_relay(
        patch_order, lengths, cond, ada, latents[0], stale_keys[0, 0], stale_values[0, 0], main, rem
    )
    return out[None, None]


def solution(mesh):
    return jax.shard_map(
        local,
        mesh=mesh,
        in_specs=(
            P("row", None, "col", None),
            P("row"),
            P("row"),
            P(),
            P("section", "row", None, "col"),
            P("section", "row", None, "col"),
            P("section", "col", "row"),
            P("section", "row", "col"),
            P("section", "col", "row"),
            P("section", "row", None, None, "col"),
            P("section", "row", None, None, "col"),
        ),
        out_specs=P("section", "row", None, "col", None),
        check_vma=False,
    )
```

```python
import math

import jax
import jax.numpy as jnp
from jax import lax
from jax.experimental import pallas as pl
from jax.experimental.pallas import tpu as pltpu
from jax.sharding import PartitionSpec as P

D = 1152
HD = 72
F32 = jnp.float32
BF16 = jnp.bfloat16

HEADW = 640
COL_OUT = 3 * HEADW
COL_UP = 4 * HEADW
COL_DOWN = COL_UP + 2304
COLS = COL_DOWN + 2304
QUARTER = COLS // 4
MODW = 6 * HEADW
ADAROWS = 48
CHUNKS = ((0, COL_UP), (COL_UP, COL_DOWN), (COL_DOWN, COLS))
MAIN = 1024
MESH = pl.DeviceIdType.MESH
NT = (((1,), (1,)), ((), ()))


def sinusoid(step_ids):
    half_width = D // 2
    frequency = jnp.exp(-math.log(10000.0) * jnp.arange(half_width, dtype=F32) / half_width)
    angles = step_ids.astype(F32)[:, None] * frequency[None, :]
    return jnp.concatenate([jnp.cos(angles), jnp.sin(angles)], axis=1)


def halves(chunk):
    start, stop = CHUNKS[chunk]
    middle = start + (stop - start) // 2
    return ((start, middle - start), (middle, stop - middle))


def relay(
    place_ref, length_ref, cond_ref, ada_ref, lat_ref, keys_ref, values_ref, main_ref, rem_ref, out_ref,
    order, mask_ref, stale_k, stale_v, latp, yout,
    cbuf, cmat, ada_got, part, got_z, sum_z, got_y, sum_y, got_x, mods, mod_ref,
    wall, stag, wrem, x, x1, qs, kbuf, vbuf, att, hid, h, pa_own, pa_got, pm_own, pm_got, y,
    give_send, give_recv, cond_send, cond_recv, sum_send, sum_recv, go_sem, local_sem, xh_send, xh_recv, send_sem, recv_sem, col_send, col_recv, pass_send, pass_recv,
):
    sec = lax.axis_index("section")
    row = lax.axis_index("row")
    col = lax.axis_index("col")
    z, yy, xh = row // 8, lax.rem(row // 2, 4), lax.rem(row, 2)

    def at(section=None, zz=None, y_=None, x_=None, c=None):
        s_ = sec if section is None else section
        r_ = ((z if zz is None else zz) * 4 + (yy if y_ is None else y_)) * 2 + (xh if x_ is None else x_)
        return (s_, r_, col if c is None else c)

    y_peer = [lax.rem(yy + d, 4) for d in range(4)]
    z_peer = [lax.rem(z + d, 4) for d in range(4)]
    xh_dev = at(x_=1 - xh)
    col_dev = at(c=1 - col)
    sec_dev = at(section=1 - sec)

    barrier = pltpu.get_barrier_semaphore()
    for dev in (
        [xh_dev, col_dev, sec_dev]
        + [at(y_=y_peer[d]) for d in (1, 2, 3)]
        + [at(zz=z_peer[d]) for d in (1, 2, 3)]
    ):
        pl.semaphore_signal(barrier, inc=1, device_id=dev, device_id_type=MESH)
    pl.semaphore_wait(barrier, 9)

    def rdma(src, dst, s_sem, r_sem, dev):
        return pltpu.make_async_remote_copy(
            src_ref=src, dst_ref=dst, send_sem=s_sem, recv_sem=r_sem, device_id=dev, device_id_type=MESH
        )

    def buf(k):
        return (stag, 16, rem_ref) if k == 0 else (wall, 32, main_ref)

    def span(k, half):
        if k == 0:
            return ((0, QUARTER // 2), (QUARTER // 2, QUARTER // 2))[half]
        return halves(k - 1)[half]

    pieces = range(1 + len(CHUNKS))

    def xh_copy(k):
        ref, rows, src = buf(k)
        c0 = span(k, 0)[0]
        width = span(k, 0)[1] + span(k, 1)[1]
        return rdma(
            src.at[:, pl.ds(c0, width)],
            ref.at[z, yy, pl.ds(xh * rows, rows), pl.ds(c0, width)],
            xh_send.at[k], xh_recv.at[k], xh_dev,
        )

    def xh_arrival(k):
        ref, rows, src = buf(k)
        c0 = span(k, 0)[0]
        width = span(k, 0)[1] + span(k, 1)[1]
        return rdma(
            src.at[:, pl.ds(c0, width)],
            ref.at[z, yy, pl.ds((1 - xh) * rows, rows), pl.ds(c0, width)],
            xh_send.at[k], xh_recv.at[k], xh_dev,
        )

    def ring_copy(k, half, phase, link, arrival):
        i = ((phase * 2 + half) * 4 + k) * 4 + link
        along_y = (half == 0) == (phase == 0)
        ahead = link % 2 == 0
        peers = y_peer if along_y else z_peer
        dev = at(y_=peers[1 if ahead else 3]) if along_y else at(zz=peers[1 if ahead else 3])
        if arrival:
            member = peers[(3 if ahead else 1) if link < 2 else 2]
        else:
            member = peers[0 if link < 2 else (3 if ahead else 1)]
        c0, width = span(k, half)
        if link >= 2:
            first = (width // 256) * 128 if (width // 128) % 2 == 0 else (width // 256 + 1) * 128
            c0, width = (c0, first) if ahead else (c0 + first, width - first)
        ref = buf(k)[0]
        zz, y_ = (z, member) if along_y else (member, yy)
        if phase == 0:
            ref = ref.at[zz, y_, :, pl.ds(c0, width)]
        elif along_y:
            ref = ref.at[:, y_, :, pl.ds(c0, width)]
        else:
            ref = ref.at[zz, :, :, pl.ds(c0, width)]
        return rdma(ref, ref, send_sem.at[i], recv_sem.at[i], dev)

    def near(k, phase):
        for half in (0, 1):
            for link in (0, 1):
                ring_copy(k, half, phase, link, False).start()

    def relay_on(k, phase):
        for half in (0, 1):
            for link in (0, 1):
                ring_copy(k, half, phase, link, True).wait_recv()
                ring_copy(k, half, phase, link + 2, False).start()

    def far_arrived(k, phase):
        for half in (0, 1):
            for link in (2, 3):
                ring_copy(k, half, phase, link, True).wait_recv()

    def go():
        @pl.when(sec == 0)
        def _():
            pl.semaphore_signal(go_sem, inc=1, device_id=sec_dev, device_id_type=MESH)

    def await_go():
        @pl.when(sec == 1)
        def _():
            pl.semaphore_wait(go_sem, 1)

    own_keys = pltpu.make_async_copy(keys_ref, stale_k, local_sem.at[3])
    own_values = pltpu.make_async_copy(values_ref, stale_v, local_sem.at[4])
    own_main = pltpu.make_async_copy(main_ref, wall.at[z, yy, pl.ds(xh * 32, 32)], local_sem.at[0])
    own_rem = pltpu.make_async_copy(rem_ref, stag.at[z, yy, pl.ds(xh * 16, 16)], local_sem.at[1])
    own_cond = pltpu.make_async_copy(cond_ref, cbuf.at[z, yy, pl.ds(xh * 32, 32)], local_sem.at[2])
    cond_xh = rdma(cond_ref, cbuf.at[z, yy, pl.ds(xh * 32, 32)], cond_send.at[0], cond_recv.at[0], xh_dev)
    own_main.start()
    own_rem.start()
    own_keys.start()
    own_values.start()
    ada_copy = rdma(ada_ref, ada_got, give_send.at[0], give_recv.at[0], sec_dev)
    mods_copy = rdma(mods.at[0], mods.at[0], give_send.at[1], give_recv.at[1], sec_dev)

    @pl.when(sec == 0)
    def _():
        ada_copy.start()

    def build_order():
        lane = lax.broadcasted_iota(jnp.int32, (128, D), 1)
        rest_lane = lane - MAIN
        source = jnp.where(
            lane < MAIN, (lane >> 5) * 36 + (lane & 31), (rest_lane >> 2) * 36 + 32 + (rest_lane & 3)
        )
        for i in range(9):
            natural = lax.broadcasted_iota(jnp.int32, (128, D), 0) + i * 128
            order[i * 128:(i + 1) * 128, :] = jnp.where(natural == source, 1.0, 0.0).astype(BF16)

    def lat_copy(j):
        return rdma(
            latp.at[j], x.at[j, pl.ds(col * 128, 128)], pass_send.at[4 + j], pass_recv.at[4 + j], col_dev
        )

    def send_piece(k):
        xh_arrival(k).wait_recv()
        near(k, 0)

    def cond_y(d, arrival):
        ref = cbuf.at[z, y_peer[4 - d] if arrival else yy]
        return rdma(ref, ref, cond_send.at[d], cond_recv.at[d], at(y_=y_peer[d]))

    def cond_z(d, arrival):
        ref = cbuf.at[z_peer[4 - d] if arrival else z]
        return rdma(ref, ref, cond_send.at[3 + d], cond_recv.at[3 + d], at(zz=z_peer[d]))

    def summing(n, src, dst, i, dev):
        return rdma(src, dst, sum_send.at[n * 8 + i], sum_recv.at[n * 8 + i], dev)

    def part_z(n, d):
        return summing(n, part.at[n, z_peer[d]], got_z.at[n, d - 1], d - 1, at(zz=z_peer[d]))

    def part_y(n, d):
        return summing(n, sum_z.at[n, y_peer[d]], got_y.at[n, d - 1], d + 2, at(y_=y_peer[d]))

    def part_x(n):
        return summing(n, sum_y.at[n, 1 - xh], got_x.at[n], 6, xh_dev)

    def mod_copy(n, c):
        return summing(n, mods.at[n, c], mods.at[n, c], 7, col_dev)

    @pl.when(sec == 1)
    def _():
        own_cond.start()
        cond_xh.start()
        own_cond.wait()
        rdma(
            cond_ref, cbuf.at[z, yy, pl.ds((1 - xh) * 32, 32)], cond_send.at[0], cond_recv.at[0], xh_dev
        ).wait_recv()
        for d in (1, 3, 2):
            cond_y(d, False).start()
        for d in (1, 3, 2):
            cond_y(d, True).wait_recv()
        for d in (1, 3, 2):
            cond_z(d, False).start()
        for d in (1, 3, 2):
            cond_z(d, True).wait_recv()
        for i in range(32):
            cmat[i:i + 1, :] = cbuf[i // 8, (i // 2) % 4, pl.ds((i % 2) * 32 + row, 1), :]
        ada_copy.wait_recv()
        for n, weight in ((0, ada_got), (1, ada_ref)):
            products = jnp.dot(
                cmat[:, :ADAROWS].astype(BF16), weight[...], preferred_element_type=F32
            )
            for i in range(32):
                part[n, i // 8, (i // 2) % 4, i % 2] = products[i:i + 1, :]
            for d in (1, 3, 2):
                part_z(n, d).start()
            for d in (1, 3, 2):
                part_z(n, d).wait_recv()
            sum_z[n] = part[n, z] + got_z[n, 0] + got_z[n, 1] + got_z[n, 2]
            for d in (1, 3, 2):
                part_y(n, d).start()
            for d in (1, 3, 2):
                part_y(n, d).wait_recv()
            sum_y[n] = sum_z[n, yy] + got_y[n, 0] + got_y[n, 1] + got_y[n, 2]
            part_x(n).start()
            part_x(n).wait_recv()
            mods[n, col] = sum_y[n, xh] + got_x[n]
            mod_copy(n, col).start()
            mod_copy(n, 1 - col).wait_recv()
            if n == 0:
                mods_copy.start()

    await_go()
    for k in pieces:
        xh_copy(k).start()
    own_main.wait()
    own_rem.wait()
    build_order()

    @pl.when(sec == 0)
    def _():
        for j in range(4):
            latp[j] = jnp.dot(lat_ref[place_ref[j]], order[...], preferred_element_type=F32).astype(BF16)
        x[:, pl.ds(col * 128, 128), :] = latp[...]

    own_keys.wait()
    own_values.wait()
    for j in range(4):
        kbuf[j, :, :576] = stale_k[place_ref[j]]
        vbuf[j, :, :576] = stale_v[place_ref[j]]
        kbuf[j, :, 576:] = jnp.zeros((256, HEADW - 576), BF16)
        vbuf[j, :, 576:] = jnp.zeros((256, HEADW - 576), BF16)
        token = lax.broadcasted_iota(jnp.int32, (1, 256), 1) + place_ref[j] * 256
        mask_ref[:, j * 256:(j + 1) * 256] = jnp.where(token < length_ref[0], 0.0, -1e30)
    att[...] = jnp.zeros_like(att)

    await_go()
    send_piece(0)
    send_piece(1)
    relay_on(0, 0)
    relay_on(1, 0)
    await_go()
    far_arrived(0, 0)
    near(0, 1)
    far_arrived(1, 0)
    near(1, 1)
    send_piece(2)
    send_piece(3)
    go()

    @pl.when(sec == 0)
    def _():
        for j in range(4):
            lat_copy(j).start()

    relay_on(2, 0)
    relay_on(3, 0)
    relay_on(0, 1)
    relay_on(1, 1)
    far_arrived(2, 0)
    near(2, 1)
    far_arrived(3, 0)
    near(3, 1)
    far_arrived(0, 1)
    rows_i = lax.broadcasted_iota(jnp.int32, (128, 512), 0)
    cols_i = lax.broadcasted_iota(jnp.int32, (128, 512), 1)
    for q in range(4):
        pick = jnp.where(
            ((cols_i >> 4) == (rows_i >> 2)) & ((cols_i & 15) == 4 * q + (rows_i & 3)), 1.0, 0.0
        ).astype(BF16)
        wrem[:, q * QUARTER:(q + 1) * QUARTER] = jnp.dot(
            pick, stag[...].reshape(512, QUARTER), preferred_element_type=F32
        ).astype(BF16)

    def norm_rows(load, shift, scale):
        def body(i, carry):
            rows = pl.ds(pl.multiple_of(i * 64, 64), 64)
            v = load(rows)
            mean = jnp.sum(v, axis=-1, keepdims=True) * (1.0 / D)
            v = v - mean
            var = jnp.sum(v * v, axis=-1, keepdims=True) * (1.0 / D)
            normed = v * lax.rsqrt(var + 1e-6)
            h[rows, :] = (normed * (1.0 + scale[...]) + shift[...]).astype(BF16)
            return carry
        lax.fori_loop(0, 4, body, 0, unroll=4)

    def times(lhs_ref, c0, width):
        return jnp.dot(
            lhs_ref[:, :MAIN], wall[:, :, :, pl.ds(c0, width)].reshape(MAIN, width), preferred_element_type=F32
        ) + jnp.dot(lhs_ref[:, MAIN:], wrem[:, pl.ds(c0, width)], preferred_element_type=F32)

    def times_t(load, dst, j, c0, width):
        dst[j, :, :MAIN] = lax.dot_general(
            load(), wall[:, :, :, pl.ds(c0, width)].reshape(MAIN, width), NT, preferred_element_type=F32
        ).astype(BF16)
        dst[j, :, MAIN:] = lax.dot_general(
            load(), wrem[:, pl.ds(c0, width)], NT, preferred_element_type=F32
        ).astype(BF16)

    def col_copy(own, got, j, base):
        return rdma(own.at[j], got.at[j], col_send.at[base + j], col_recv.at[base + j], col_dev)

    def pass_copy(j):
        return rdma(y.at[j], x.at[j], pass_send.at[j], pass_recv.at[j], sec_dev)

    def half_copy(j):
        part_rows = pl.ds((1 - col) * 128, 128)
        return rdma(
            pm_own.at[j, part_rows], pm_got.at[j, part_rows], col_send.at[4 + j], col_recv.at[4 + j], col_dev
        )

    def mlp_copy(j, act):
        @pl.when(sec == 0)
        def _():
            act(col_copy(pm_own, pm_got, j, 4))

        @pl.when(sec == 1)
        def _():
            act(half_copy(j))

    @pl.when(sec == 0)
    def _():
        mods_copy.wait_recv()
    for k in range(6):
        base = k * HEADW
        for c in (0, 1):
            mod_ref[k:k + 1, c * 512:(c + 1) * 512] = mods[sec, c, :, base:base + 512]
        mod_ref[k:k + 1, MAIN:] = (
            mods[sec, 0, :, base + 512:base + HEADW] + mods[sec, 1, :, base + 512:base + HEADW]
        )

    far_arrived(1, 1)

    def attend_step(j):
        @pl.when(sec == 0)
        def _():
            lat_copy(j).wait_recv()

        @pl.when(sec == 1)
        def _():
            pass_copy(j).wait_recv()

        norm_rows(lambda rows: x[j, rows, :].astype(F32), mod_ref.at[0:1], mod_ref.at[1:2])
        qkv = times(h, 0, 3 * HEADW).astype(BF16)
        qs[...] = qkv[:, :HEADW]
        kbuf[j] = qkv[:, HEADW:2 * HEADW]
        vbuf[j] = qkv[:, 2 * HEADW:]

        def heads(p, c):
            window = pl.ds(pl.multiple_of(p * 128, 128), 256)
            q_win = qs[:, window]
            k_win = kbuf[:, :, window].reshape(1024, 256)
            v_win = vbuf[:, :, window].reshape(1024, 256)
            lane = lax.broadcasted_iota(jnp.int32, (256, 256), 1) - p * 16
            mixed = att[:, window].astype(F32)
            for e in (0, 1):
                mine = (lane >= e * HD) & (lane < (e + 1) * HD)
                scores = lax.dot_general(
                    jnp.where(mine, q_win.astype(F32), 0.0).astype(BF16), k_win, NT, preferred_element_type=F32
                ) * (math.log2(math.e) / math.sqrt(HD)) + mask_ref[...]
                weights = jnp.exp2(scores - jnp.max(scores, axis=-1, keepdims=True))
                totals = jnp.sum(weights, axis=-1, keepdims=True)
                got = jnp.dot(weights.astype(BF16), v_win, preferred_element_type=F32)
                mixed = jnp.where(mine, got * (1.0 / totals), mixed)
            att[:, window] = mixed.astype(BF16)
            return c
        lax.fori_loop(0, 4, heads, 0, unroll=4)
        times_t(lambda: att[...], pa_own, j, COL_OUT, HEADW)
        col_copy(pa_own, pa_got, j, 0).start()

    def mlp_step(j):
        col_copy(pa_own, pa_got, j, 0).wait_recv()

        def load(rows):
            v = x[j, rows, :].astype(F32) + mod_ref[2:3] * (
                pa_own[j, rows, :].astype(F32) + pa_got[j, rows, :].astype(F32)
            )
            x1[j, rows, :] = v
            return v
        norm_rows(load, mod_ref.at[3:4], mod_ref.at[4:5])

        def body(n, c):
            u = times(h, pl.multiple_of(COL_UP + n * 768, 256), 768)
            g = 0.5 * u * (1.0 + jnp.tanh(math.sqrt(2.0 / math.pi) * (u + 0.044715 * (u * u * u))))
            hid[:, pl.ds(pl.multiple_of(n * 768, 256), 768)] = g.astype(BF16)
            return c
        lax.fori_loop(0, 3, body, 0, unroll=3)
        times_t(lambda: hid[...], pm_own, j, COL_DOWN, 2304)
        mlp_copy(j, lambda copy: copy.start())

    def finish(j):
        mlp_copy(j, lambda copy: copy.wait_recv())

        def settle(i):
            rows = pl.ds(pl.multiple_of(i * 64, 64), 64)
            y[j, rows, :] = (
                x1[j, rows, :]
                + mod_ref[5:6] * (pm_own[j, rows, :].astype(F32) + pm_got[j, rows, :].astype(F32))
            ).astype(BF16)

        @pl.when(sec == 0)
        def _():
            lax.fori_loop(0, 4, lambda i, c: settle(i) or c, 0)
            pass_copy(j).start()

        @pl.when(sec == 1)
        def _():
            lax.fori_loop(0, 2, lambda i, c: settle(col * 2 + i) or c, 0)
        yout[j] = lax.dot_general(
            y[j, pl.ds(col * 128, 128), :], order[...], NT, preferred_element_type=F32
        ).astype(BF16)

    def first_half(t, carry):
        attend_step(t)

        @pl.when(t == 0)
        def _():
            relay_on(2, 1)
            relay_on(3, 1)
            go()
            go()
        return carry
    lax.fori_loop(0, 4, first_half, 0)
    far_arrived(2, 1)
    far_arrived(3, 1)

    def second_half(t, carry):
        mlp_step(t)

        @pl.when(t > 0)
        def _():
            finish(t - 1)
        return carry
    lax.fori_loop(0, 4, second_half, 0)
    finish(3)
    for p in range(4):
        slot = jnp.int32(0)
        for j in range(1, 4):
            slot = jnp.where(place_ref[j] == p, j, slot)
        out_ref[p] = yout[slot]

    @pl.when(sec == 0)
    def _():
        ada_copy.wait_send()

    @pl.when(sec == 1)
    def _():
        cond_xh.wait_send()
        for d in (1, 2, 3):
            cond_y(d, False).wait_send()
            cond_z(d, False).wait_send()
            for n in (0, 1):
                part_z(n, d).wait_send()
                part_y(n, d).wait_send()
        for n in (0, 1):
            part_x(n).wait_send()
            mod_copy(n, col).wait_send()
        mods_copy.wait_send()

    for k in pieces:
        xh_copy(k).wait_send()
        for phase in (0, 1):
            for half in (0, 1):
                for link in range(4):
                    ring_copy(k, half, phase, link, False).wait_send()

    def drain(j, c):
        col_copy(pa_own, pa_got, j, 0).wait_send()
        mlp_copy(j, lambda copy: copy.wait_send())

        @pl.when(sec == 0)
        def _():
            pass_copy(j).wait_send()
            lat_copy(j).wait_send()
        return c
    lax.fori_loop(0, 4, drain, 0)


def run_relay(place, length, cond, ada, lat, stale_k, stale_v, main, rem):
    vmem = pl.BlockSpec(memory_space=pltpu.VMEM)
    tokens = (4, 256, D)
    return pl.pallas_call(
        relay,
        out_shape=jax.ShapeDtypeStruct((4, 128, D), BF16),
        in_specs=[pl.BlockSpec(memory_space=pltpu.SMEM)] * 2 + [vmem] * 3 + [pl.BlockSpec(memory_space=pltpu.HBM)] * 2 + [vmem] * 2,
        out_specs=vmem,
        scratch_shapes=[
            pltpu.VMEM((D, D), BF16),
            pltpu.VMEM((1, 1024), F32),
            pltpu.VMEM((4, 256, 576), BF16),
            pltpu.VMEM((4, 256, 576), BF16),
            pltpu.VMEM((4, 128, D), BF16),
            pltpu.VMEM((4, 128, D), BF16),
            pltpu.VMEM((4, 4, 64, 128), F32),
            pltpu.VMEM((32, 128), F32),
            pltpu.VMEM((ADAROWS, MODW), BF16),
            pltpu.VMEM((2, 4, 4, 2, 1, MODW), F32),
            pltpu.VMEM((2, 3, 4, 2, 1, MODW), F32),
            pltpu.VMEM((2, 4, 2, 1, MODW), F32),
            pltpu.VMEM((2, 3, 2, 1, MODW), F32),
            pltpu.VMEM((2, 2, 1, MODW), F32),
            pltpu.VMEM((2, 1, MODW), F32),
            pltpu.VMEM((2, 2, 1, MODW), F32),
            pltpu.VMEM((8, D), F32),
            pltpu.VMEM((4, 4, 64, COLS), BF16),
            pltpu.VMEM((4, 4, 32, QUARTER), BF16),
            pltpu.VMEM((128, COLS), BF16),
            pltpu.VMEM(tokens, BF16),
            pltpu.VMEM(tokens, F32),
            pltpu.VMEM((256, HEADW), BF16),
            pltpu.VMEM((4, 256, HEADW), BF16),
            pltpu.VMEM((4, 256, HEADW), BF16),
            pltpu.VMEM((256, HEADW), BF16),
            pltpu.VMEM((256, 2304), BF16),
            pltpu.VMEM((256, D), BF16),
            pltpu.VMEM(tokens, BF16),
            pltpu.VMEM(tokens, BF16),
            pltpu.VMEM(tokens, BF16),
            pltpu.VMEM(tokens, BF16),
            pltpu.VMEM(tokens, BF16),
            pltpu.SemaphoreType.DMA((2,)),
            pltpu.SemaphoreType.DMA((2,)),
            pltpu.SemaphoreType.DMA((7,)),
            pltpu.SemaphoreType.DMA((7,)),
            pltpu.SemaphoreType.DMA((16,)),
            pltpu.SemaphoreType.DMA((16,)),
            pltpu.SemaphoreType.REGULAR,
            pltpu.SemaphoreType.DMA((5,)),
            pltpu.SemaphoreType.DMA((4,)),
            pltpu.SemaphoreType.DMA((4,)),
            pltpu.SemaphoreType.DMA((64,)),
            pltpu.SemaphoreType.DMA((64,)),
            pltpu.SemaphoreType.DMA((8,)),
            pltpu.SemaphoreType.DMA((8,)),
            pltpu.SemaphoreType.DMA((8,)),
            pltpu.SemaphoreType.DMA((8,)),
        ],
        compiler_params=pltpu.CompilerParams(
            collective_id=0, has_side_effects=True, vmem_limit_bytes=67043328
        ),
    )(place, length, cond, ada, lat, stale_k, stale_v, main, rem)


def local(
    latents,
    timesteps,
    lengths,
    patch_order,
    ada_weight,
    qkv_weight,
    out_weight,
    up_weight,
    down_weight,
    stale_keys,
    stale_values,
):
    cond = jax.nn.silu(sinusoid(timesteps)).astype(BF16).astype(F32)
    cond = jnp.pad(cond.reshape(32, 36), ((0, 0), (0, 92)))
    from_col = jnp.arange(576, dtype=jnp.int32)
    group, inner = from_col // 36, from_col % 36
    to_col = jnp.where(
        inner < 32, group * 32 + inner, 512 + 64 * lax.axis_index("col") + group * 4 + inner - 32
    )
    spread = (to_col[:, None] == jnp.arange(HEADW, dtype=jnp.int32)[None, :]).astype(BF16)
    ada = jnp.einsum("dkc,ce->dke", ada_weight[0], spread, preferred_element_type=F32).astype(BF16)
    ada = jnp.pad(ada.reshape(36, MODW), ((0, ADAROWS - 36), (0, 0)))

    pad = lambda a, n: jnp.pad(a, ((0, 0), (0, n - a.shape[1])))
    shard = jnp.concatenate(
        [pad(qkv_weight[0, :, i], HEADW) for i in range(3)]
        + [pad(out_weight[0].T, HEADW), up_weight[0], down_weight[0].T],
        axis=1,
    )
    main = shard[:32]
    rem = shard[32:].reshape(4, 4, QUARTER).transpose(1, 0, 2).reshape(16, QUARTER)

    out = run_relay(
        patch_order, lengths, cond, ada, latents[0], stale_keys[0, 0], stale_values[0, 0], main, rem
    )
    return out[None, None]


def solution(mesh):
    return jax.shard_map(
        local,
        mesh=mesh,
        in_specs=(
            P("row", None, "col", None),
            P("row"),
            P("row"),
            P(),
            P("section", "row", None, "col"),
            P("section", "row", None, "col"),
            P("section", "col", "row"),
            P("section", "row", "col"),
            P("section", "col", "row"),
            P("section", "row", None, None, "col"),
            P("section", "row", None, None, "col"),
        ),
        out_specs=P("section", "row", None, "col", None),
        check_vma=False,
    )
```
